32 devices in a mesh: groups: 2 (over y), vocab: 8 (over z, x), mp: 2 (over core).
Axes of the slice: x: 2, y: 2, z: 4, core: 2. Of those that a mesh axis runs over, the one named last changes fastest.
Arguments:
- gate_pre: bfloat16 [32, 14336], P(('groups', 'vocab'), 'mp'), parts along dimension 0, may hold values from -6 to 6
- up_pre: bfloat16 [32, 14336], P(('groups', 'vocab'), 'mp'), parts along dimension 0, may hold values from -6 to 6
- down_weight: bfloat16 [8192, 14336], P('vocab', 'mp'), may hold values from -0.046875 to 0.046875
- residual: bfloat16 [32, 8192], P(('groups', 'vocab', 'mp')), parts along dimension 0, may hold values from -36 to 36
- norm_gain: bfloat16 [8192], replicated, may hold values from 0.5 to 1.5
- head_weight: bfloat16 [8192, 4032], P('mp', 'vocab')
- targets: int32 [32], P(('groups', 'mp')), parts along dimension 0, may hold values from 0 to 4031
Outputs:
- log_likelihood: float32 [32], P(('groups', 'mp')), parts along dimension 0
The draws below stay inside these ranges and needn't reach their ends.
There are 2 independent parts, one for each index of `groups`. The reference program is written for one: setup_inputs(seed, part) draws one part's arguments, and reference() takes and returns one part's arrays. A program takes and returns all parts, laid end to end along the dimension named above; an argument that names none is the same for every part. Nothing has to cross between parts.
All inputs are finite; a program needn't handle non-finite values.
Results may differ from the reference program's by a relative error of at most 0.0003.
The reference program's roundings to bfloat16 on the way (of `gated_units`, `stream` and `normed`) count: a program that leaves them out, or rounds other values in their place, can miss the bound.
Values may be sent and summed in bfloat16 or wider, within the bound.
No kernel may reach another device: no remote copies, remote signals or barrier semaphores. Data moves between devices by JAX's collectives and lax.ppermute only.
A program may use at most 64 MiB of HBM per device.

```python
import math
import jax
import jax.numpy as jnp
from jax import lax

D = 8192
FF = 14336
TOKENS = 16
VOCAB = 4032


def draw_residual(key, part):
    subkeys = jax.random.split(key, 3)
    row_scale = jnp.exp(jax.random.uniform(subkeys[0], (TOKENS, 1), jnp.float32, math.log(0.3), math.log(3.0)))
    column_scale = jnp.exp(jax.random.uniform(subkeys[1], (1, D), jnp.float32, math.log(0.3), math.log(3.0)))
    rough_part = jnp.clip(jax.random.normal(subkeys[2], (TOKENS, D), jnp.float32), -4.0, 4.0)
    return (rough_part * row_scale * column_scale).astype(jnp.bfloat16)


def draw_head_weight(key, part):
    subkeys = jax.random.split(key, 2)
    rising = 1.2 + 1.2 * jnp.arange(VOCAB, dtype=jnp.float32) / VOCAB
    spread = jnp.exp(jax.random.uniform(subkeys[1], (VOCAB,), jnp.float32, 0.0, math.log(3.0)))
    scales = (spread * rising)[None, :] / math.sqrt(D)
    noise_draw = jnp.clip(jax.random.normal(subkeys[0], (D, VOCAB), jnp.float32), -4.0, 4.0)
    return (noise_draw * scales).astype(jnp.bfloat16)


def with_ends(drawn, key, low, largest):
    place = [jax.random.randint(jax.random.fold_in(key, axis), (), 0, length) for axis, length in enumerate(drawn.shape)]
    longest = drawn.shape.index(max(drawn.shape))
    beside = place[:longest] + [(place[longest] + 1) % drawn.shape[longest]] + place[longest + 1:]
    return drawn.at[tuple(place)].set(low).at[tuple(beside)].set(largest)


def steps_of(rng, extent, cuts, low, top_value):
    level = 1.0
    for dim, shards_of in cuts:
        steps = jax.random.uniform(jax.random.fold_in(jax.random.fold_in(rng, 6), dim), (shards_of,), jnp.float32, low / len(cuts), top_value / len(cuts))
        level = level * jnp.repeat(jnp.exp(steps), extent[dim] // shards_of).reshape((-1,) + (1,) * (len(extent) - 1 - dim))
    return level


def normal_values(stream_key, extent, width, reach, shards=(), held_as=jnp.bfloat16):
    values = width * jax.random.normal(stream_key, extent, jnp.float32)
    if shards:
        values = values * steps_of(stream_key, extent, shards, -0.22, 0.18)
    return jnp.clip(values, -reach, reach).astype(held_as)


def setup_inputs(seed: int = 0, part: int = 0) -> dict:
    key_list = jax.random.split(jax.random.key(seed), 8)
    own_keys = jax.random.split(jax.random.fold_in(key_list[7], part), 8)
    gate_pre = normal_values(own_keys[0], (TOKENS, FF), 1.0, 6.0, ((0, 8), (1, 2)))
    up_pre = normal_values(own_keys[1], (TOKENS, FF), 1.0, 6.0, ((0, 8), (1, 2)))
    down_weight = normal_values(key_list[2], (D, FF), FF ** -0.5, 0.046875, ((0, 8), (1, 2)))
    residual = draw_residual(jax.random.fold_in(jax.random.fold_in(key_list[7], part), 71), part)
    norm_gain = jnp.clip(1.0 + 0.1 * jax.random.normal(key_list[4], (D,), jnp.float32), 0.5, 1.5).astype(jnp.bfloat16)
    head_weight = draw_head_weight(jax.random.fold_in(key_list[7], 71), part)
    targets = with_ends(jax.random.randint(own_keys[6], (TOKENS,), 0, VOCAB), jax.random.fold_in(own_keys[6], 1), 0, VOCAB - 1).astype(jnp.int32)
    return {"gate_pre": gate_pre, "up_pre": up_pre, "down_weight": down_weight, "residual": residual, "norm_gain": norm_gain, "head_weight": head_weight, "targets": targets}


def reference(gate_pre, up_pre, down_weight, residual, norm_gain, head_weight, targets):
    gated_units = (jax.nn.silu(gate_pre.astype(jnp.float32)) * up_pre.astype(jnp.float32)).astype(jnp.bfloat16)
    update = lax.dot_general(gated_units, down_weight, (((1,), (1,)), ((), ())), preferred_element_type=jnp.float32)
    stream = (residual.astype(jnp.float32) + update).astype(jnp.bfloat16)
    stream = lax.optimization_barrier(stream)
    widened = stream.astype(jnp.float32)
    mean_square = lax.optimization_barrier(jnp.mean(widened * widened, axis=1, keepdims=True))
    normed = (widened * lax.rsqrt(mean_square + 1e-05) * norm_gain.astype(jnp.float32)[None, :]).astype(jnp.bfloat16)
    logits = jnp.dot(normed, head_weight, preferred_element_type=jnp.float32)
    row_top = lax.optimization_barrier(jnp.max(logits, axis=1))
    exp_total = lax.optimization_barrier(jnp.sum(jnp.exp(logits - row_top[:, None]), axis=1))
    columns = lax.broadcasted_iota(jnp.int32, logits.shape, 1)
    chosen = lax.optimization_barrier(jnp.sum(jnp.where(columns == targets.astype(jnp.int32)[:, None], logits, 0.0), axis=1))
    return chosen - row_top - jnp.log(exp_total)
```

```python
import jax
import jax.numpy as jnp
from jax import lax
from jax.sharding import PartitionSpec as P

EPSILON = 1e-05


def spread(value, axis):
    count = lax.axis_size(axis)
    copies = jnp.broadcast_to(value[None], (count,) + value.shape)
    return lax.all_to_all(copies, axis, 0, 0, tiled=True)


def partner(value):
    return lax.ppermute(value, "mp", [(0, 1), (1, 0)])


def body(gate_pre, up_pre, down_weight, residual, norm_gain, head_weight, targets):
    vocab_count = lax.axis_size("vocab")
    model_index = lax.axis_index("mp")
    vocab_index = lax.axis_index("vocab")
    rows, half_units = gate_pre.shape
    block = down_weight.shape[0]
    own_rows = residual.shape[0]
    tokens = rows * vocab_count
    gated_units = (jax.nn.silu(gate_pre.astype(jnp.float32)) * up_pre.astype(jnp.float32)).astype(
        jnp.bfloat16
    )
    extra = own_rows * block // rows
    blocks = residual.reshape(own_rows, vocab_count, block).transpose(1, 0, 2)
    sent = jnp.concatenate(
        [
            jnp.broadcast_to(gated_units[None], (vocab_count, rows, half_units)),
            blocks.reshape(vocab_count, rows, extra),
        ],
        axis=2,
    )
    arrived = lax.all_to_all(sent, "vocab", 0, 0, tiled=True)
    units = arrived[:, :, :half_units].reshape(tokens, half_units)
    own_residual = arrived[:, :, half_units:].reshape(vocab_count, 1, own_rows, block)
    down_terms = lax.dot_general(
        units, down_weight, (((1,), (1,)), ((), ())), preferred_element_type=jnp.float32
    )
    mine = lax.broadcasted_iota(jnp.int32, (1, rows // own_rows, 1, 1), 1) == model_index
    terms = down_terms.reshape(vocab_count, rows // own_rows, own_rows, block) + jnp.where(
        mine, own_residual.astype(jnp.float32), 0.0
    )
    terms = terms.reshape(tokens, block)
    stream = (terms + partner(terms)).astype(jnp.bfloat16)
    stream = lax.optimization_barrier(stream)
    whole = spread(stream, "vocab")
    widened = whole.astype(jnp.float32)
    width = vocab_count * block
    mean_square = jnp.sum(widened * widened, axis=(0, 2)) / width
    half_width = head_weight.shape[0]
    half_blocks = vocab_count // lax.axis_size("mp")
    here = lax.dynamic_slice_in_dim(whole, model_index * half_blocks, half_blocks, 0)
    gain = lax.dynamic_slice_in_dim(norm_gain, model_index * half_width, half_width, 0)
    normed = (
        here.astype(jnp.float32)
        * lax.rsqrt(mean_square + EPSILON)[None, :, None]
        * gain.astype(jnp.float32).reshape(half_blocks, 1, block)
    ).astype(jnp.bfloat16)
    normed = normed.transpose(1, 0, 2).reshape(tokens, half_width)
    logit_terms = jnp.dot(normed, head_weight, preferred_element_type=jnp.float32)
    half_tokens = targets.shape[0]
    kept = lax.dynamic_slice_in_dim(logit_terms, model_index * half_tokens, half_tokens, 0)
    given = lax.dynamic_slice_in_dim(logit_terms, (1 - model_index) * half_tokens, half_tokens, 0)
    logits = kept + partner(given)
    local_ids = targets - vocab_index * logits.shape[1]
    columns = lax.broadcasted_iota(jnp.int32, logits.shape, 1)
    chosen = jnp.sum(jnp.where(columns == local_ids[:, None], logits, 0.0), axis=1)
    row_top = jnp.max(logits, axis=1)
    exp_total = jnp.sum(jnp.exp(logits - row_top[:, None]), axis=1)
    stats = spread(jnp.stack([row_top, exp_total, chosen]), "vocab")
    top = jnp.max(stats[:, 0], axis=0)
    total = jnp.sum(stats[:, 1] * jnp.exp(stats[:, 0] - top[None]), axis=0)
    return jnp.sum(stats[:, 2], axis=0) - top - jnp.log(total)


def solution(mesh):
    return jax.shard_map(
        body,
        mesh=mesh,
        in_specs=(
            P(("groups", "vocab"), "mp"),
            P(("groups", "vocab"), "mp"),
            P("vocab", "mp"),
            P(("groups", "vocab", "mp"), None),
            P(),
            P("mp", "vocab"),
            P(("groups", "mp")),
        ),
        out_specs=P(("groups", "mp")),
        check_vma=False,
    )
```

```python
import jax
import jax.numpy as jnp
from jax import lax
from jax.experimental import pallas as pl
from jax.experimental.pallas import tpu as pltpu
from jax.sharding import PartitionSpec as P

EPSILON = 1e-05
ROWS_BY_ROWS = (((1,), (1,)), ((), ()))
SMALL = 2 << 20
fence = lax.optimization_barrier
NEAR = pl.BlockSpec(memory_space=pltpu.VMEM)
FAR = pl.BlockSpec(memory_space=pltpu.HBM)
VECTOR = pltpu.VMEM
DMA = pltpu.SemaphoreType.DMA


def partner(value):
    return lax.ppermute(value, "mp", [(0, 1), (1, 0)])


def swapped(value):
    return fence(lax.all_to_all(fence(value), "vocab", 0, 0, tiled=True))


def call(kernel, out_shape, operands, places, scratch=(), grant=SMALL):
    operands = tuple(
        pltpu.with_memory_space_constraint(one, pltpu.HBM) if place is FAR else one
        for one, place in zip(operands, places)
    )
    return pl.pallas_call(
        kernel,
        out_shape=out_shape,
        in_specs=places,
        out_specs=jax.tree.map(lambda _: NEAR, out_shape),
        scratch_shapes=list(scratch),
        compiler_params=pltpu.CompilerParams(vmem_limit_bytes=grant),
    )(*operands)


def pieces(length, most, step):
    for count in range(pl.cdiv(length, most), length + 1):
        if length % count == 0 and (length // count) % step == 0:
            return count
    return 1


def gated_kernel(gate_hbm, up_hbm, residual_hbm, out_ref, gate_ref, up_ref, residual_ref, done):
    loads = (
        pltpu.make_async_copy(gate_hbm, gate_ref, done.at[0]),
        pltpu.make_async_copy(up_hbm, up_ref, done.at[1]),
        pltpu.make_async_copy(residual_hbm, residual_ref, done.at[2]),
    )
    for load in loads:
        load.start()
    for load in loads:
        load.wait()
    count, rows, width = out_ref.shape
    units = gate_ref.shape[1]
    block = width - units
    gate = gate_ref[...].astype(jnp.float32)
    up = up_ref[...].astype(jnp.float32)
    gated = (gate / (1.0 + jnp.exp(-gate)) * up).astype(jnp.bfloat16)
    token = lax.broadcasted_iota(jnp.int32, (rows, block), 0)
    first = lax.axis_index("mp") * residual_ref.shape[0]
    for peer in range(count):
        out_ref[peer, :, :units] = gated
        tail = jnp.zeros((rows, block), jnp.float32)
        for row in range(residual_ref.shape[0]):
            here = residual_ref[row : row + 1, peer * block : (peer + 1) * block]
            here = jnp.broadcast_to(here.astype(jnp.float32), (rows, block))
            tail = jnp.where(token == first + row, here, tail)
        out_ref[peer, :, units:] = tail.astype(jnp.bfloat16)


def weight_loads(weight_hbm, weight_ref, done, row_parts, unit_parts):
    rows, units = weight_ref.shape[0] // row_parts, weight_ref.shape[1] // unit_parts
    loads = {}
    for i in range(row_parts):
        for j in range(unit_parts):
            here = (pl.ds(i * rows, rows), pl.ds(j * units, units))
            loads[i, j] = pltpu.make_async_copy(
                weight_hbm.at[here], weight_ref.at[here], done.at[i, j]
            )
            loads[i, j].start()
    return loads, rows, units


def down_kernel(parts, chunks_ref, weight_hbm, kept_ref, given_ref, weight_ref, units_ref, done):
    loads, block, depth = weight_loads(weight_hbm, weight_ref, done, *parts)
    count, rows, width = chunks_ref.shape
    units = weight_ref.shape[1]
    half = kept_ref.shape[0]
    for peer in range(count):
        units_ref[peer * rows : (peer + 1) * rows, :] = chunks_ref[peer]
    is_low = lax.axis_index("mp") == 0
    for i in range(parts[0]):
        here = slice(i * block, (i + 1) * block)
        terms = units_ref[:, units + i * block : units + (i + 1) * block].astype(jnp.float32)
        for j in range(parts[1]):
            loads[i, j].wait()
            deep = slice(j * depth, (j + 1) * depth)
            terms += lax.dot_general(
                units_ref[:, deep],
                weight_ref[here, deep],
                ROWS_BY_ROWS,
                preferred_element_type=jnp.float32,
            )
        low, high = terms[:half], terms[half:]
        kept_ref[:, here] = jnp.where(is_low, low, high)
        given_ref[:, here] = jnp.where(is_low, high, low)


def stream_kernel(kept_ref, arrived_ref, out_ref):
    stream = (kept_ref[...] + arrived_ref[...]).astype(jnp.bfloat16)
    for peer in range(out_ref.shape[0]):
        out_ref[peer] = stream


def norm_kernel(stream_ref, gain_ref, own_ref, other_ref):
    count, tokens, block = stream_ref.shape
    half = count // 2
    squares = jnp.zeros((tokens, block), jnp.float32)
    for part in range(count):
        values = stream_ref[part].astype(jnp.float32)
        squares += values * values
    mean_square = jnp.sum(squares, axis=1, keepdims=True) / (count * block)
    scale = lax.rsqrt(mean_square + EPSILON)
    index = lax.axis_index("mp")
    for out_ref, side in ((own_ref, index), (other_ref, 1 - index)):
        for part in range(half):
            at = side * half + part
            gain = gain_ref[pl.ds(at, 1), :]
            values = stream_ref[at].astype(jnp.float32) * scale * gain
            out_ref[:, part * block : (part + 1) * block] = values.astype(jnp.bfloat16)


def head_kernel(parts, own_ref, other_ref, weight_hbm, kept_ref, given_ref, weight_ref, done):
    loads, block, depth = weight_loads(weight_hbm, weight_ref, done, *parts)
    tokens = own_ref.shape[0]
    terms = jnp.zeros((2 * tokens, block), jnp.float32)
    for j in range(parts[1]):
        loads[0, j].wait()
        deep = slice(j * depth, (j + 1) * depth)
        terms += lax.dot_general(
            jnp.concatenate([own_ref[:, deep], other_ref[:, deep]], axis=0),
            weight_ref[:, deep],
            ROWS_BY_ROWS,
            preferred_element_type=jnp.float32,
        )
    kept_ref[...] = terms[:tokens]
    given_ref[...] = terms[tokens:]


def body(gate_pre, up_pre, down_weight, residual, norm_gain, head_weight, targets):
    vocab_count = lax.axis_size("vocab")
    vocab_index = lax.axis_index("vocab")
    rows, half_units = gate_pre.shape
    block = down_weight.shape[0]
    tokens = rows * vocab_count
    half_tokens = targets.shape[0]
    half_width, columns_here = head_weight.shape
    shaped = jax.ShapeDtypeStruct
    chunk = shaped((vocab_count, rows, half_units + block), jnp.bfloat16)
    operands = (gate_pre, up_pre, residual)
    places = [VECTOR(one.shape, one.dtype) for one in operands]
    chunks = swapped(call(gated_kernel, chunk, operands, [FAR] * 3, places + [DMA((3,))]))
    part = shaped((half_tokens, block), jnp.float32)
    parts = (pieces(block, 256, 8), pieces(half_units, 1792, 128))
    kept, given = call(
        lambda *refs: down_kernel(parts, *refs),
        (part, part),
        (chunks, down_weight),
        [NEAR, FAR],
        [
            VECTOR(down_weight.shape, jnp.bfloat16),
            VECTOR((tokens, half_units + block), jnp.bfloat16),
            DMA(parts),
        ],
        24 << 20,
    )
    chunk = shaped((vocab_count, half_tokens, block), jnp.bfloat16)
    gain = norm_gain.astype(jnp.float32).reshape(vocab_count, block)
    arrived, gain = fence((partner(given), gain))
    stream = swapped(call(stream_kernel, chunk, (kept, arrived), [NEAR] * 2))
    part = shaped((half_tokens, half_width), jnp.bfloat16)
    own, other = call(norm_kernel, (part, part), (stream, gain), [NEAR] * 2)
    part = shaped((half_tokens, columns_here), jnp.float32)
    parts_head = (1, pieces(half_width, 1024, 128))
    kept, given = call(
        lambda *refs: head_kernel(parts_head, *refs),
        (part, part),
        (own, partner(other), head_weight.T),
        [NEAR, NEAR, FAR],
        [VECTOR((columns_here, half_width), jnp.bfloat16), DMA(parts_head)],
        12 << 20,
    )
    logits = kept + partner(given)
    local_ids = targets - vocab_index * columns_here
    columns = lax.broadcasted_iota(jnp.int32, logits.shape, 1)
    chosen = jnp.sum(jnp.where(columns == local_ids[:, None], logits, 0.0), axis=1)
    row_top = jnp.max(logits, axis=1)
    exp_total = jnp.sum(jnp.exp(logits - row_top[:, None]), axis=1)
    stats = jnp.stack([row_top, exp_total, chosen])
    stats = swapped(jnp.broadcast_to(stats[None], (vocab_count,) + stats.shape))
    top = jnp.max(stats[:, 0], axis=0)
    total = jnp.sum(stats[:, 1] * jnp.exp(stats[:, 0] - top[None]), axis=0)
    return jnp.sum(stats[:, 2], axis=0) - top - jnp.log(total)


def solution(mesh):
    return jax.shard_map(
        body,
        mesh=mesh,
        in_specs=(
            P(("groups", "vocab"), "mp"),
            P(("groups", "vocab"), "mp"),
            P("vocab", "mp"),
            P(("groups", "vocab", "mp"), None),
            P(),
            P("mp", "vocab"),
            P(("groups", "mp")),
        ),
        out_specs=P(("groups", "mp")),
        check_vma=False,
    )
```

```python
import jax
import jax.numpy as jnp
from jax import lax
from jax.experimental import pallas as pl
from jax.experimental.pallas import tpu as pltpu
from jax.sharding import PartitionSpec as P

EPSILON = 1e-05
ROWS_BY_ROWS = (((1,), (1,)), ((), ()))
SMALL = 2 << 20
GRANT = 8 << 20
fence = lax.optimization_barrier
NEAR = pl.BlockSpec(memory_space=pltpu.VMEM)
FAR = pl.BlockSpec(memory_space=pltpu.HBM)
VECTOR = pltpu.VMEM
DMA = pltpu.SemaphoreType.DMA


def brought(weight):
    own = [(k, k) for k in range(lax.axis_size("mp"))]
    return pltpu.with_memory_space_constraint(lax.ppermute(weight, "mp", own), pltpu.VMEM)


def partner(value):
    return lax.ppermute(value, "mp", [(0, 1), (1, 0)])


def swapped(value):
    return fence(lax.all_to_all(fence(value), "vocab", 0, 0, tiled=True))


def call(kernel, out_shape, operands, places, scratch=(), grant=SMALL):
    operands = tuple(
        pltpu.with_memory_space_constraint(one, pltpu.HBM) if place is FAR else one
        for one, place in zip(operands, places)
    )
    return pl.pallas_call(
        kernel,
        out_shape=out_shape,
        in_specs=places,
        out_specs=jax.tree.map(lambda _: NEAR, out_shape),
        scratch_shapes=list(scratch),
        compiler_params=pltpu.CompilerParams(vmem_limit_bytes=grant),
    )(*operands)


def pieces(length, most, step):
    for count in range(pl.cdiv(length, most), length + 1):
        if length % count == 0 and (length // count) % step == 0:
            return count
    return 1


def gated_kernel(gate_hbm, up_hbm, residual_hbm, out_ref, gate_ref, up_ref, residual_ref, done):
    loads = (
        pltpu.make_async_copy(gate_hbm, gate_ref, done.at[0]),
        pltpu.make_async_copy(up_hbm, up_ref, done.at[1]),
        pltpu.make_async_copy(residual_hbm, residual_ref, done.at[2]),
    )
    for load in loads:
        load.start()
    for load in loads:
        load.wait()
    count, rows, width = out_ref.shape
    units = gate_ref.shape[1]
    block = width - units
    gate = gate_ref[...].astype(jnp.float32)
    up = up_ref[...].astype(jnp.float32)
    gated = (gate / (1.0 + jnp.exp(-gate)) * up).astype(jnp.bfloat16)
    token = lax.broadcasted_iota(jnp.int32, (rows, block), 0)
    first = lax.axis_index("mp") * residual_ref.shape[0]
    for peer in range(count):
        out_ref[peer, :, :units] = gated
        tail = jnp.zeros((rows, block), jnp.float32)
        for row in range(residual_ref.shape[0]):
            here = residual_ref[row : row + 1, peer * block : (peer + 1) * block]
            here = jnp.broadcast_to(here.astype(jnp.float32), (rows, block))
            tail = jnp.where(token == first + row, here, tail)
        out_ref[peer, :, units:] = tail.astype(jnp.bfloat16)


def down_kernel(chunks_ref, weight_ref, kept_ref, given_ref, units_ref):
    count, rows, width = chunks_ref.shape
    units = weight_ref.shape[1]
    half = kept_ref.shape[0]
    for peer in range(count):
        units_ref[peer * rows : (peer + 1) * rows, :] = chunks_ref[peer]
    terms = lax.dot_general(
        units_ref[:, :units], weight_ref[...], ROWS_BY_ROWS, preferred_element_type=jnp.float32
    ) + units_ref[:, units:].astype(jnp.float32)
    low, high = terms[:half], terms[half:]
    is_low = lax.axis_index("mp") == 0
    kept_ref[...] = jnp.where(is_low, low, high)
    given_ref[...] = jnp.where(is_low, high, low)


def stream_kernel(kept_ref, arrived_ref, out_ref):
    stream = (kept_ref[...] + arrived_ref[...]).astype(jnp.bfloat16)
    for peer in range(out_ref.shape[0]):
        out_ref[peer] = stream


def norm_kernel(stream_ref, gain_ref, own_ref, other_ref):
    count, tokens, block = stream_ref.shape
    half = count // 2
    squares = jnp.zeros((tokens, block), jnp.float32)
    for part in range(count):
        values = stream_ref[part].astype(jnp.float32)
        squares += values * values
    mean_square = jnp.sum(squares, axis=1, keepdims=True) / (count * block)
    scale = lax.rsqrt(mean_square + EPSILON)
    index = lax.axis_index("mp")
    for out_ref, side in ((own_ref, index), (other_ref, 1 - index)):
        for part in range(half):
            at = side * half + part
            gain = gain_ref[pl.ds(at, 1), :]
            values = stream_ref[at].astype(jnp.float32) * scale * gain
            out_ref[:, part * block : (part + 1) * block] = values.astype(jnp.bfloat16)


def weight_loads(weight_hbm, weight_ref, done, row_parts, unit_parts):
    rows, units = weight_ref.shape[0] // row_parts, weight_ref.shape[1] // unit_parts
    loads = {}
    for i in range(row_parts):
        for j in range(unit_parts):
            here = (pl.ds(i * rows, rows), pl.ds(j * units, units))
            loads[i, j] = pltpu.make_async_copy(
                weight_hbm.at[here], weight_ref.at[here], done.at[i, j]
            )
            loads[i, j].start()
    return loads, rows, units


def head_kernel(parts, own_ref, other_ref, weight_hbm, kept_ref, given_ref, weight_ref, done):
    loads, block, depth = weight_loads(weight_hbm, weight_ref, done, *parts)
    tokens = own_ref.shape[0]
    terms = jnp.zeros((2 * tokens, block), jnp.float32)
    for j in range(parts[1]):
        loads[0, j].wait()
        deep = slice(j * depth, (j + 1) * depth)
        terms += lax.dot_general(
            jnp.concatenate([own_ref[:, deep], other_ref[:, deep]], axis=0),
            weight_ref[:, deep],
            ROWS_BY_ROWS,
            preferred_element_type=jnp.float32,
        )
    kept_ref[...] = terms[:tokens]
    given_ref[...] = terms[tokens:]


def body(gate_pre, up_pre, down_weight, residual, norm_gain, head_weight, targets):
    vocab_count = lax.axis_size("vocab")
    vocab_index = lax.axis_index("vocab")
    rows, half_units = gate_pre.shape
    block = down_weight.shape[0]
    tokens = rows * vocab_count
    half_tokens = targets.shape[0]
    half_width, columns_here = head_weight.shape
    shaped = jax.ShapeDtypeStruct
    down_rows = brought(down_weight)
    chunk = shaped((vocab_count, rows, half_units + block), jnp.bfloat16)
    operands = (gate_pre, up_pre, residual)
    places = [VECTOR(one.shape, one.dtype) for one in operands]
    chunks = swapped(call(gated_kernel, chunk, operands, [FAR] * 3, places + [DMA((3,))]))
    part = shaped((half_tokens, block), jnp.float32)
    kept, given = call(
        down_kernel,
        (part, part),
        (chunks, down_rows),
        [NEAR, NEAR],
        [VECTOR((tokens, half_units + block), jnp.bfloat16)],
        GRANT,
    )
    chunk = shaped((vocab_count, half_tokens, block), jnp.bfloat16)
    gain = norm_gain.astype(jnp.float32).reshape(vocab_count, block)
    arrived, gain = fence((partner(given), gain))
    stream = swapped(call(stream_kernel, chunk, (kept, arrived), [NEAR] * 2))
    part = shaped((half_tokens, half_width), jnp.bfloat16)
    own, other = call(norm_kernel, (part, part), (stream, gain), [NEAR] * 2)
    part = shaped((half_tokens, columns_here), jnp.float32)
    parts_head = (1, pieces(half_width, 512, 128))
    kept, given = call(
        lambda *refs: head_kernel(parts_head, *refs),
        (part, part),
        (own, partner(other), head_weight.T),
        [NEAR, NEAR, FAR],
        [VECTOR((columns_here, half_width), jnp.bfloat16), DMA(parts_head)],
        12 << 20,
    )
    logits = kept + partner(given)
    local_ids = targets - vocab_index * columns_here
    columns = lax.broadcasted_iota(jnp.int32, logits.shape, 1)
    chosen = jnp.sum(jnp.where(columns == local_ids[:, None], logits, 0.0), axis=1)
    row_top = jnp.max(logits, axis=1)
    exp_total = jnp.sum(jnp.exp(logits - row_top[:, None]), axis=1)
    stats = jnp.stack([row_top, exp_total, chosen])
    stats = swapped(jnp.broadcast_to(stats[None], (vocab_count,) + stats.shape))
    top = jnp.max(stats[:, 0], axis=0)
    total = jnp.sum(stats[:, 1] * jnp.exp(stats[:, 0] - top[None]), axis=0)
    return jnp.sum(stats[:, 2], axis=0) - top - jnp.log(total)


def solution(mesh):
    return jax.shard_map(
        body,
        mesh=mesh,
        in_specs=(
            P(("groups", "vocab"), "mp"),
            P(("groups", "vocab"), "mp"),
            P("vocab", "mp"),
            P(("groups", "vocab", "mp"), None),
            P(),
            P("mp", "vocab"),
            P(("groups", "mp")),
        ),
        out_specs=P(("groups", "mp")),
        check_vma=False,
    )
```

```python
import jax
import jax.numpy as jnp
from jax import lax
from jax.experimental import pallas as pl
from jax.experimental.pallas import tpu as pltpu
from jax.sharding import PartitionSpec as P

EPSILON = 1e-05
ROWS_BY_ROWS = (((1,), (1,)), ((), ()))
SMALL = 2 << 20
fence = lax.optimization_barrier
NEAR = pl.BlockSpec(memory_space=pltpu.VMEM)
FAR = pl.BlockSpec(memory_space=pltpu.HBM)
VECTOR = pltpu.VMEM
DMA = pltpu.SemaphoreType.DMA


def partner(value):
    return lax.ppermute(value, "mp", [(0, 1), (1, 0)])


def swapped(value):
    return fence(lax.all_to_all(fence(value), "vocab", 0, 0, tiled=True))


def call(kernel, out_shape, operands, places, scratch=(), grant=SMALL):
    operands = tuple(
        pltpu.with_memory_space_constraint(one, pltpu.HBM) if place is FAR else one
        for one, place in zip(operands, places)
    )
    return pl.pallas_call(
        kernel,
        out_shape=out_shape,
        in_specs=places,
        out_specs=jax.tree.map(lambda _: NEAR, out_shape),
        scratch_shapes=list(scratch),
        compiler_params=pltpu.CompilerParams(vmem_limit_bytes=grant),
    )(*operands)


def pieces(length, most, step):
    for count in range(pl.cdiv(length, most), length + 1):
        if length % count == 0 and (length // count) % step == 0:
            return count
    return 1


def gated_kernel(gate_hbm, up_hbm, residual_hbm, out_ref, gate_ref, up_ref, residual_ref, done):
    loads = (
        pltpu.make_async_copy(gate_hbm, gate_ref, done.at[0]),
        pltpu.make_async_copy(up_hbm, up_ref, done.at[1]),
        pltpu.make_async_copy(residual_hbm, residual_ref, done.at[2]),
    )
    for load in loads:
        load.start()
    for load in loads:
        load.wait()
    count, rows, width = out_ref.shape
    units = gate_ref.shape[1]
    block = width - units
    gate = gate_ref[...].astype(jnp.float32)
    up = up_ref[...].astype(jnp.float32)
    gated = (gate / (1.0 + jnp.exp(-gate)) * up).astype(jnp.bfloat16)
    token = lax.broadcasted_iota(jnp.int32, (rows, block), 0)
    first = lax.axis_index("mp") * residual_ref.shape[0]
    for peer in range(count):
        out_ref[peer, :, :units] = gated
        tail = jnp.zeros((rows, block), jnp.float32)
        for row in range(residual_ref.shape[0]):
            here = residual_ref[row : row + 1, peer * block : (peer + 1) * block]
            here = jnp.broadcast_to(here.astype(jnp.float32), (rows, block))
            tail = jnp.where(token == first + row, here, tail)
        out_ref[peer, :, units:] = tail.astype(jnp.bfloat16)


def weight_loads(weight_hbm, weight_ref, done, row_parts, unit_parts):
    rows, units = weight_ref.shape[0] // row_parts, weight_ref.shape[1] // unit_parts
    loads = {}
    for i in range(row_parts):
        for j in range(unit_parts):
            here = (pl.ds(i * rows, rows), pl.ds(j * units, units))
            loads[i, j] = pltpu.make_async_copy(
                weight_hbm.at[here], weight_ref.at[here], done.at[i, j]
            )
            loads[i, j].start()
    return loads, rows, units


def down_kernel(parts, chunks_ref, weight_hbm, kept_ref, given_ref, weight_ref, units_ref, done):
    loads, block, depth = weight_loads(weight_hbm, weight_ref, done, *parts)
    count, rows, width = chunks_ref.shape
    units = weight_ref.shape[1]
    half = kept_ref.shape[0]
    for peer in range(count):
        units_ref[peer * rows : (peer + 1) * rows, :] = chunks_ref[peer]
    is_low = lax.axis_index("mp") == 0
    for i in range(parts[0]):
        here = slice(i * block, (i + 1) * block)
        terms = units_ref[:, units + i * block : units + (i + 1) * block].astype(jnp.float32)
        for j in range(parts[1]):
            loads[i, j].wait()
            deep = slice(j * depth, (j + 1) * depth)
            terms += lax.dot_general(
                units_ref[:, deep],
                weight_ref[here, deep],
                ROWS_BY_ROWS,
                preferred_element_type=jnp.float32,
            )
        low, high = terms[:half], terms[half:]
        kept_ref[:, here] = jnp.where(is_low, low, high)
        given_ref[:, here] = jnp.where(is_low, high, low)


def stream_kernel(kept_ref, arrived_ref, out_ref):
    stream = (kept_ref[...] + arrived_ref[...]).astype(jnp.bfloat16)
    for peer in range(out_ref.shape[0]):
        out_ref[peer] = stream


def norm_kernel(stream_ref, gain_ref, own_ref, other_ref):
    count, tokens, block = stream_ref.shape
    half = count // 2
    squares = jnp.zeros((tokens, block), jnp.float32)
    for part in range(count):
        values = stream_ref[part].astype(jnp.float32)
        squares += values * values
    mean_square = jnp.sum(squares, axis=1, keepdims=True) / (count * block)
    scale = lax.rsqrt(mean_square + EPSILON)
    index = lax.axis_index("mp")
    for out_ref, side in ((own_ref, index), (other_ref, 1 - index)):
        for part in range(half):
            at = side * half + part
            gain = gain_ref[pl.ds(at, 1), :]
            values = stream_ref[at].astype(jnp.float32) * scale * gain
            out_ref[:, part * block : (part + 1) * block] = values.astype(jnp.bfloat16)


def head_kernel(parts, own_ref, other_ref, weight_hbm, kept_ref, given_ref, weight_ref, done):
    loads, block, depth = weight_loads(weight_hbm, weight_ref, done, *parts)
    tokens = own_ref.shape[0]
    terms = jnp.zeros((2 * tokens, block), jnp.float32)
    for j in range(parts[1]):
        loads[0, j].wait()
        deep = slice(j * depth, (j + 1) * depth)
        terms += lax.dot_general(
            jnp.concatenate([own_ref[:, deep], other_ref[:, deep]], axis=0),
            weight_ref[:, deep],
            ROWS_BY_ROWS,
            preferred_element_type=jnp.float32,
        )
    kept_ref[...] = terms[:tokens]
    given_ref[...] = terms[tokens:]


def stats_kernel(kept_ref, arrived_ref, targets_ref, out_ref):
    logits = kept_ref[...] + arrived_ref[...]
    tokens, columns = logits.shape
    square = (tokens, tokens)
    diagonal = lax.broadcasted_iota(jnp.int32, square, 0) == lax.broadcasted_iota(
        jnp.int32, square, 1
    )
    wanted = jnp.broadcast_to(targets_ref[...].reshape(1, tokens), square).astype(jnp.float32)
    wanted = jnp.sum(jnp.where(diagonal, wanted, 0.0), axis=1, keepdims=True).astype(jnp.int32)
    wanted -= lax.axis_index("vocab") * columns
    here = lax.broadcasted_iota(jnp.int32, logits.shape, 1) == wanted
    chosen = jnp.sum(jnp.where(here, logits, 0.0), axis=1, keepdims=True)
    top = jnp.max(logits, axis=1, keepdims=True)
    total = jnp.sum(jnp.exp(logits - top), axis=1, keepdims=True)
    lane = lax.broadcasted_iota(jnp.int32, (tokens, 3 * tokens), 1)
    token = lax.broadcasted_iota(jnp.int32, (tokens, 3 * tokens), 0)
    row = jnp.zeros((tokens, 3 * tokens), jnp.float32)
    for place, value in enumerate((top, total, chosen)):
        row = jnp.where(lane == token + place * tokens, value, row)
    row = jnp.sum(row, axis=0, keepdims=True)
    for peer in range(out_ref.shape[0]):
        out_ref[peer] = row


def merge_kernel(stats_ref, out_ref):
    tokens = out_ref.shape[1]
    tops = stats_ref[:, 0, :tokens]
    totals = stats_ref[:, 0, tokens : 2 * tokens]
    chosen = jnp.sum(stats_ref[:, 0, 2 * tokens :], axis=0, keepdims=True)
    top = jnp.max(tops, axis=0, keepdims=True)
    total = jnp.sum(totals * jnp.exp(tops - top), axis=0, keepdims=True)
    out_ref[...] = chosen - top - jnp.log(total)


def body(gate_pre, up_pre, down_weight, residual, norm_gain, head_weight, targets):
    vocab_count = lax.axis_size("vocab")
    rows, half_units = gate_pre.shape
    block = down_weight.shape[0]
    tokens = rows * vocab_count
    half_tokens = targets.shape[0]
    half_width, columns_here = head_weight.shape
    shaped = jax.ShapeDtypeStruct
    chunk = shaped((vocab_count, rows, half_units + block), jnp.bfloat16)
    operands = (gate_pre, up_pre, residual)
    places = [VECTOR(one.shape, one.dtype) for one in operands]
    chunks = swapped(call(gated_kernel, chunk, operands, [FAR] * 3, places + [DMA((3,))]))
    part = shaped((half_tokens, block), jnp.float32)
    parts = (1, pieces(half_units, 512, 128))
    kept, given = call(
        lambda *refs: down_kernel(parts, *refs),
        (part, part),
        (chunks, down_weight),
        [NEAR, FAR],
        [
            VECTOR(down_weight.shape, jnp.bfloat16),
            VECTOR((tokens, half_units + block), jnp.bfloat16),
            DMA(parts),
        ],
        24 << 20,
    )
    chunk = shaped((vocab_count, half_tokens, block), jnp.bfloat16)
    gain = norm_gain.astype(jnp.float32).reshape(vocab_count, block)
    arrived, gain = fence((partner(given), gain))
    stream = swapped(call(stream_kernel, chunk, (kept, arrived), [NEAR] * 2))
    part = shaped((half_tokens, half_width), jnp.bfloat16)
    own, other = call(norm_kernel, (part, part), (stream, gain), [NEAR] * 2)
    part = shaped((half_tokens, columns_here), jnp.float32)
    parts_head = (1, pieces(half_width, 512, 128))
    kept, given = call(
        lambda *refs: head_kernel(parts_head, *refs),
        (part, part),
        (own, partner(other), head_weight.T),
        [NEAR, NEAR, FAR],
        [VECTOR((columns_here, half_width), jnp.bfloat16), DMA(parts_head)],
        12 << 20,
    )
    row = shaped((vocab_count, 1, 3 * half_tokens), jnp.float32)
    operands = (kept, partner(given), targets)
    stats = swapped(call(stats_kernel, row, operands, [NEAR] * 3))
    row = shaped((1, half_tokens), jnp.float32)
    return call(merge_kernel, row, (stats,), [NEAR]).reshape(half_tokens)


def solution(mesh):
    return jax.shard_map(
        body,
        mesh=mesh,
        in_specs=(
            P(("groups", "vocab"), "mp"),
            P(("groups", "vocab"), "mp"),
            P("vocab", "mp"),
            P(("groups", "vocab", "mp"), None),
            P(),
            P("mp", "vocab"),
            P(("groups", "mp")),
        ),
        out_specs=P(("groups", "mp")),
        check_vma=False,
    )
```

```python
import jax
import jax.numpy as jnp
from jax import lax
from jax.experimental import pallas as pl
from jax.experimental.pallas import tpu as pltpu
from jax.sharding import PartitionSpec as P

EPSILON = 1e-05
ROWS_BY_ROWS = (((1,), (1,)), ((), ()))
SMALL = 2 << 20
fence = lax.optimization_barrier
NEAR = pl.BlockSpec(memory_space=pltpu.VMEM)
FAR = pl.BlockSpec(memory_space=pltpu.HBM)
FREE = pl.BlockSpec(memory_space=pl.ANY)
VECTOR = pltpu.VMEM
DMA = pltpu.SemaphoreType.DMA


def partner(value):
    return lax.ppermute(value, "mp", [(0, 1), (1, 0)])


def swapped(value):
    return fence(lax.all_to_all(fence(value), "vocab", 0, 0, tiled=True))


def call(
    kernel, out_shape, operands, places, scratch=(), results=None, grant=SMALL, cost=0
):
    operands = tuple(
        pltpu.with_memory_space_constraint(one, pltpu.HBM) if place is FAR else one
        for one, place in zip(operands, places)
    )
    return pl.pallas_call(
        kernel,
        out_shape=out_shape,
        in_specs=places,
        out_specs=results or jax.tree.map(lambda _: NEAR, out_shape),
        scratch_shapes=list(scratch),
        cost_estimate=pl.CostEstimate(flops=0, bytes_accessed=cost, transcendentals=0) if cost else None,
        compiler_params=pltpu.CompilerParams(vmem_limit_bytes=grant),
    )(*operands)


def block_of(length, most):
    return max(size for size in range(1, most + 1) if length % size == 0)


def gated_kernel(
    gate_hbm, up_hbm, residual_hbm, weight_hbm, out_ref, early_ref, gate_ref, up_ref, residual_ref, done
):
    loads = (
        pltpu.make_async_copy(gate_hbm, gate_ref, done.at[0]),
        pltpu.make_async_copy(up_hbm, up_ref, done.at[1]),
        pltpu.make_async_copy(residual_hbm, residual_ref, done.at[2]),
        pltpu.make_async_copy(
            weight_hbm.at[:, pl.ds(0, early_ref.shape[1])], early_ref, done.at[3]
        ),
    )
    for load in loads:
        load.start()
    for load in loads[:3]:
        load.wait()
    count, rows, width = out_ref.shape
    units = gate_ref.shape[1]
    extra = width - units
    gate = gate_ref[...].astype(jnp.float32)
    up = up_ref[...].astype(jnp.float32)
    gated = (gate / (1.0 + jnp.exp(-gate)) * up).astype(jnp.bfloat16)
    for peer in range(count):
        out_ref[peer, :, :units] = gated
        for row in range(rows):
            first = (peer * rows + row) * extra
            out_ref[peer, row : row + 1, units:] = residual_ref[:, first : first + extra]
    loads[3].wait()


def weight_loads(weight_hbm, weight_ref, done, skip):
    depth = weight_ref.shape[1] // done.shape[0]
    loads = []
    for part in range(done.shape[0]):
        loads.append(
            pltpu.make_async_copy(
                weight_hbm.at[:, pl.ds(skip + part * depth, depth)],
                weight_ref.at[:, pl.ds(part * depth, depth)],
                done.at[part],
            )
        )
        loads[-1].start()
    return loads, depth


def product(left, early_ref, weight_ref, loads, depth):
    skip = early_ref.shape[1]
    terms = lax.dot_general(
        left(0, skip), early_ref[...], ROWS_BY_ROWS, preferred_element_type=jnp.float32
    )
    for part, load in enumerate(loads):
        load.wait()
        terms += lax.dot_general(
            left(skip + part * depth, depth),
            weight_ref[:, part * depth : (part + 1) * depth],
            ROWS_BY_ROWS,
            preferred_element_type=jnp.float32,
        )
    return terms


def down_kernel(chunks_ref, early_ref, weight_hbm, kept_ref, given_ref, weight_ref, units_ref, done):
    units = weight_hbm.shape[1]
    loads, depth = weight_loads(weight_hbm, weight_ref, done, early_ref.shape[1])
    count, rows, width = chunks_ref.shape
    half, block = kept_ref.shape
    for peer in range(count):
        units_ref[peer * rows : (peer + 1) * rows, :] = chunks_ref[peer]
    terms = product(
        lambda first, size: units_ref[:, first : first + size], early_ref, weight_ref, loads, depth
    )
    index = lax.axis_index("mp")
    token = lax.broadcasted_iota(jnp.int32, (count * rows, block), 0)
    pieces = [
        jnp.concatenate(
            [chunks_ref[peer, row : row + 1, units:].astype(jnp.float32) for row in range(rows)],
            axis=1,
        )
        for peer in range(count)
    ]
    own = jnp.concatenate([jnp.broadcast_to(piece, (rows, block)) for piece in pieces], axis=0)
    terms += jnp.where(lax.rem(token, rows) == index, own, 0.0)
    low, high = terms[:half], terms[half:]
    is_low = index == 0
    kept_ref[...] = jnp.where(is_low, low, high)
    given_ref[...] = jnp.where(is_low, high, low)


def stream_kernel(kept_ref, arrived_ref, out_ref):
    stream = (kept_ref[...] + arrived_ref[...]).astype(jnp.bfloat16)
    for peer in range(out_ref.shape[0]):
        out_ref[peer] = stream


def norm_kernel(stream_ref, gain_ref, own_ref, other_ref):
    count, tokens, block = stream_ref.shape
    half = count // 2
    squares = jnp.zeros((tokens, block), jnp.float32)
    for part in range(count):
        values = stream_ref[part].astype(jnp.float32)
        squares += values * values
    mean_square = jnp.sum(squares, axis=1, keepdims=True) / (count * block)
    scale = lax.rsqrt(mean_square + EPSILON)
    index = lax.axis_index("mp")
    for out_ref, side in ((own_ref, index), (other_ref, 1 - index)):
        for part in range(half):
            at = side * half + part
            gain = gain_ref[pl.ds(at, 1), :]
            values = stream_ref[at].astype(jnp.float32) * scale * gain
            out_ref[:, part * block : (part + 1) * block] = values.astype(jnp.bfloat16)


def early_kernel(weight_hbm, early_ref, done):
    load = pltpu.make_async_copy(weight_hbm.at[:, pl.ds(0, early_ref.shape[1])], early_ref, done)
    load.start()
    load.wait()


def head_kernel(own_ref, other_ref, early_ref, weight_hbm, kept_ref, given_ref, weight_ref, done):
    loads, depth = weight_loads(weight_hbm, weight_ref, done, early_ref.shape[1])
    tokens = own_ref.shape[0]
    terms = product(
        lambda first, size: jnp.concatenate(
            [own_ref[:, first : first + size], other_ref[:, first : first + size]], axis=0
        ),
        early_ref,
        weight_ref,
        loads,
        depth,
    )
    kept_ref[...] = terms[:tokens]
    given_ref[...] = terms[tokens:]


def stats_kernel(kept_ref, arrived_ref, targets_ref, out_ref):
    logits = kept_ref[...] + arrived_ref[...]
    tokens, columns = logits.shape
    square = (tokens, tokens)
    diagonal = lax.broadcasted_iota(jnp.int32, square, 0) == lax.broadcasted_iota(
        jnp.int32, square, 1
    )
    wanted = jnp.broadcast_to(targets_ref[...].reshape(1, tokens), square).astype(jnp.float32)
    wanted = jnp.sum(jnp.where(diagonal, wanted, 0.0), axis=1, keepdims=True).astype(jnp.int32)
    wanted -= lax.axis_index("vocab") * columns
    here = lax.broadcasted_iota(jnp.int32, logits.shape, 1) == wanted
    chosen = jnp.sum(jnp.where(here, logits, 0.0), axis=1, keepdims=True)
    top = jnp.max(logits, axis=1, keepdims=True)
    total = jnp.sum(jnp.exp(logits - top), axis=1, keepdims=True)
    lane = lax.broadcasted_iota(jnp.int32, (tokens, 3 * tokens), 1)
    token = lax.broadcasted_iota(jnp.int32, (tokens, 3 * tokens), 0)
    row = jnp.zeros((tokens, 3 * tokens), jnp.float32)
    for place, value in enumerate((top, total, chosen)):
        row = jnp.where(lane == token + place * tokens, value, row)
    row = jnp.sum(row, axis=0, keepdims=True)
    for peer in range(out_ref.shape[0]):
        out_ref[peer] = row


def body(gate_pre, up_pre, down_weight, residual, norm_gain, head_weight, targets):
    vocab_count = lax.axis_size("vocab")
    rows, half_units = gate_pre.shape
    block = down_weight.shape[0]
    tokens = rows * vocab_count
    half_tokens = targets.shape[0]
    half_width, columns_here = head_weight.shape
    shaped = jax.ShapeDtypeStruct
    step = block_of(half_units, 512)
    extra = residual.shape[0] * block // rows
    chunk = shaped((vocab_count, rows, half_units + extra), jnp.bfloat16)
    operands = (gate_pre, up_pre, residual, down_weight)
    places = [VECTOR(one.shape, one.dtype) for one in operands[:3]]
    early = pltpu.VMEM((block, step), jnp.bfloat16)
    chunks, early = call(
        gated_kernel, (chunk, early), operands, [FAR] * 4, places + [DMA((4,))], results=(NEAR, FREE)
    )
    part = shaped((half_tokens, block), jnp.float32)
    rest = half_units - step
    kept, given = call(
        down_kernel,
        (part, part),
        (swapped(chunks), early, down_weight),
        [NEAR, NEAR, FAR],
        [
            VECTOR((block, rest), jnp.bfloat16),
            VECTOR((tokens, half_units + extra), jnp.bfloat16),
            DMA((rest // step,)),
        ],
        grant=24 << 20,
    )
    chunk = shaped((vocab_count, half_tokens, block), jnp.bfloat16)
    gain = norm_gain.astype(jnp.float32).reshape(vocab_count, block)
    arrived, gain = fence((partner(given), gain))
    stream = swapped(call(stream_kernel, chunk, (kept, arrived), [NEAR] * 2))
    part = shaped((half_tokens, half_width), jnp.bfloat16)
    own, other = call(norm_kernel, (part, part), (stream, gain), [NEAR] * 2)
    step = block_of(half_width, 512)
    first = half_width // step // 2 * step
    other, head_weight = fence((other, head_weight))
    early = call(
        early_kernel,
        pltpu.VMEM((columns_here, first), jnp.bfloat16),
        (head_weight.T,),
        [FAR],
        [DMA],
        results=FREE,
        cost=first * columns_here * 4,
    )
    part = shaped((half_tokens, columns_here), jnp.float32)
    rest = half_width - first
    kept, given = call(
        head_kernel,
        (part, part),
        (own, partner(other), early, head_weight.T),
        [NEAR, NEAR, NEAR, FAR],
        [VECTOR((columns_here, rest), jnp.bfloat16), DMA((rest // step,))],
        grant=12 << 20,
    )
    row = shaped((vocab_count, 1, 3 * half_tokens), jnp.float32)
    operands = (kept, partner(given), targets)
    stats = swapped(call(stats_kernel, row, operands, [NEAR] * 3))
    tops, totals, chosen = jnp.split(stats[:, 0], 3, axis=1)
    top = jnp.max(tops, axis=0)
    total = jnp.sum(totals * jnp.exp(tops - top[None]), axis=0)
    return jnp.sum(chosen, axis=0) - top - jnp.log(total)


def solution(mesh):
    return jax.shard_map(
        body,
        mesh=mesh,
        in_specs=(
            P(("groups", "vocab"), "mp"),
            P(("groups", "vocab"), "mp"),
            P("vocab", "mp"),
            P(("groups", "vocab", "mp"), None),
            P(),
            P("mp", "vocab"),
            P(("groups", "mp")),
        ),
        out_specs=P(("groups", "mp")),
        check_vma=False,
    )
```

```python
import jax
import jax.numpy as jnp
from jax import lax
from jax.experimental import pallas as pl
from jax.experimental.pallas import tpu as pltpu
from jax.sharding import PartitionSpec as P

EPSILON = 1e-05
ROWS_BY_ROWS = (((1,), (1,)), ((), ()))
SMALL = 2 << 20
fence = lax.optimization_barrier
NEAR = pl.BlockSpec(memory_space=pltpu.VMEM)
FAR = pl.BlockSpec(memory_space=pltpu.HBM)
VECTOR = pltpu.VMEM
DMA = pltpu.SemaphoreType.DMA


def partner(value):
    return lax.ppermute(value, "mp", [(0, 1), (1, 0)])


def swapped(value):
    return fence(lax.all_to_all(fence(value), "vocab", 0, 0, tiled=True))


def call(kernel, out_shape, operands, places, scratch=(), grant=SMALL):
    operands = tuple(
        pltpu.with_memory_space_constraint(one, pltpu.HBM) if place is FAR else one
        for one, place in zip(operands, places)
    )
    return pl.pallas_call(
        kernel,
        out_shape=out_shape,
        in_specs=places,
        out_specs=jax.tree.map(lambda _: NEAR, out_shape),
        scratch_shapes=list(scratch),
        compiler_params=pltpu.CompilerParams(vmem_limit_bytes=grant),
    )(*operands)


def block_of(length, most):
    return max(size for size in range(1, most + 1) if length % size == 0)


def gated_kernel(gate_hbm, up_hbm, residual_hbm, out_ref, gate_ref, up_ref, residual_ref, done):
    loads = (
        pltpu.make_async_copy(gate_hbm, gate_ref, done.at[0]),
        pltpu.make_async_copy(up_hbm, up_ref, done.at[1]),
        pltpu.make_async_copy(residual_hbm, residual_ref, done.at[2]),
    )
    for load in loads:
        load.start()
    for load in loads:
        load.wait()
    count, rows, width = out_ref.shape
    units = gate_ref.shape[1]
    extra = width - units
    gate = gate_ref[...].astype(jnp.float32)
    up = up_ref[...].astype(jnp.float32)
    gated = (gate / (1.0 + jnp.exp(-gate)) * up).astype(jnp.bfloat16)
    for peer in range(count):
        out_ref[peer, :, :units] = gated
        for row in range(rows):
            first = (peer * rows + row) * extra
            out_ref[peer, row : row + 1, units:] = residual_ref[:, first : first + extra]


def weight_loads(weight_hbm, weight_ref, done):
    depth = weight_ref.shape[1] // done.shape[0]
    loads = []
    for part in range(done.shape[0]):
        here = (slice(None), pl.ds(part * depth, depth))
        loads.append(
            pltpu.make_async_copy(weight_hbm.at[here], weight_ref.at[here], done.at[part])
        )
        loads[-1].start()
    return loads


def product(terms, left_ref, weight_ref, loads):
    depth = weight_ref.shape[1] // len(loads)
    for part, load in enumerate(loads):
        load.wait()
        here = slice(part * depth, (part + 1) * depth)
        terms += lax.dot_general(
            left_ref[:, here],
            weight_ref[:, here],
            ROWS_BY_ROWS,
            preferred_element_type=jnp.float32,
        )
    return terms


def down_kernel(chunks_ref, weight_hbm, kept_ref, given_ref, weight_ref, units_ref, own_ref, done):
    loads = weight_loads(weight_hbm, weight_ref, done)
    units = weight_hbm.shape[1]
    count, rows, width = chunks_ref.shape
    half, block = kept_ref.shape
    index = lax.axis_index("mp")
    token = lax.broadcasted_iota(jnp.int32, (rows, block), 0)
    for peer in range(count):
        units_ref[peer * rows : (peer + 1) * rows, :] = chunks_ref[peer, :, :units]
        pieces = [chunks_ref[peer, row : row + 1, units:].astype(jnp.float32) for row in range(rows)]
        residual = jnp.broadcast_to(jnp.concatenate(pieces, axis=1), (rows, block))
        own_ref[peer * rows : (peer + 1) * rows, :] = jnp.where(token == index, residual, 0.0)
    terms = product(own_ref[...], units_ref, weight_ref, loads)
    low, high = terms[:half], terms[half:]
    kept_ref[...] = jnp.where(index == 0, low, high)
    given_ref[...] = jnp.where(index == 0, high, low)


def stream_kernel(kept_ref, arrived_ref, out_ref):
    stream = (kept_ref[...] + arrived_ref[...]).astype(jnp.bfloat16)
    for peer in range(out_ref.shape[0]):
        out_ref[peer] = stream


def norm_kernel(stream_ref, gain_ref, own_ref, other_ref):
    count, tokens, block = stream_ref.shape
    half = count // 2
    squares = jnp.zeros((tokens, block), jnp.float32)
    for part in range(count):
        values = stream_ref[part].astype(jnp.float32)
        squares += values * values
    mean_square = jnp.sum(squares, axis=1, keepdims=True) / (count * block)
    scale = lax.rsqrt(mean_square + EPSILON)
    index = lax.axis_index("mp")
    for out_ref, side in ((own_ref, index), (other_ref, 1 - index)):
        for part in range(half):
            at = side * half + part
            gain = gain_ref[pl.ds(at, 1), :]
            values = stream_ref[at].astype(jnp.float32) * scale * gain
            out_ref[:, part * block : (part + 1) * block] = values.astype(jnp.bfloat16)


def column_of(row_ref):
    size = row_ref.shape[0]
    square = (size, size)
    diagonal = lax.broadcasted_iota(jnp.int32, square, 0) == lax.broadcasted_iota(
        jnp.int32, square, 1
    )
    spread = jnp.broadcast_to(row_ref[...].reshape(1, size), square).astype(jnp.float32)
    return jnp.sum(jnp.where(diagonal, spread, 0.0), axis=1, keepdims=True)


def head_kernel(own_ref, other_ref, targets_ref, weight_hbm, out_ref, weight_ref, halves_ref, done):
    loads = weight_loads(weight_hbm, weight_ref, done)
    tokens = own_ref.shape[0]
    columns = weight_ref.shape[0]
    halves_ref[...] = jnp.concatenate([own_ref[...], other_ref[...]], axis=0)
    out_ref[:tokens, columns:] = column_of(targets_ref)
    out_ref[tokens:, columns:] = jnp.zeros((tokens, 1), jnp.float32)
    terms = jnp.zeros((2 * tokens, columns), jnp.float32)
    out_ref[:, :columns] = product(terms, halves_ref, weight_ref, loads)


def stats_kernel(mine_ref, arrived_ref, out_ref):
    half = mine_ref.shape[0] // 2
    columns = mine_ref.shape[1] - 1
    own = mine_ref[:half, :] + arrived_ref[half:, :]
    other = mine_ref[half:, :] + arrived_ref[:half, :]
    is_low = lax.axis_index("mp") == 0
    both = jnp.concatenate(
        [jnp.where(is_low, own, other), jnp.where(is_low, other, own)], axis=0
    )
    logits, wanted = both[:, :columns], both[:, columns:].astype(jnp.int32)
    tokens = 2 * half
    wanted -= lax.axis_index("vocab") * columns
    here = lax.broadcasted_iota(jnp.int32, logits.shape, 1) == wanted
    chosen = jnp.sum(jnp.where(here, logits, 0.0), axis=1, keepdims=True)
    top = jnp.max(logits, axis=1, keepdims=True)
    total = jnp.sum(jnp.exp(logits - top), axis=1, keepdims=True)
    lane = lax.broadcasted_iota(jnp.int32, (tokens, 3 * tokens), 1)
    token = lax.broadcasted_iota(jnp.int32, (tokens, 3 * tokens), 0)
    row = jnp.zeros((tokens, 3 * tokens), jnp.float32)
    for place, value in enumerate((top, total, chosen)):
        row = jnp.where(lane == token + place * tokens, value, row)
    row = jnp.sum(row, axis=0, keepdims=True)
    for peer in range(out_ref.shape[0]):
        out_ref[peer] = row


def body(gate_pre, up_pre, down_weight, residual, norm_gain, head_weight, targets):
    vocab_count = lax.axis_size("vocab")
    rows, half_units = gate_pre.shape
    block = down_weight.shape[0]
    tokens = rows * vocab_count
    half_tokens = targets.shape[0]
    half_width, columns_here = head_weight.shape
    shaped = jax.ShapeDtypeStruct
    step = block_of(half_units, 512)
    extra = residual.shape[0] * block // rows
    chunk = shaped((vocab_count, rows, half_units + extra), jnp.bfloat16)
    operands = (gate_pre, up_pre, residual)
    places = [VECTOR(one.shape, one.dtype) for one in operands]
    chunks = swapped(call(gated_kernel, chunk, operands, [FAR] * 3, places + [DMA((3,))]))
    part = shaped((half_tokens, block), jnp.float32)
    kept, given = call(
        down_kernel,
        (part, part),
        (chunks, down_weight),
        [NEAR, FAR],
        [
            VECTOR(down_weight.shape, jnp.bfloat16),
            VECTOR((tokens, half_units), jnp.bfloat16),
            VECTOR((tokens, block), jnp.float32),
            DMA((half_units // step,)),
        ],
        grant=24 << 20,
    )
    chunk = shaped((vocab_count, half_tokens, block), jnp.bfloat16)
    gain = norm_gain.astype(jnp.float32).reshape(vocab_count, block)
    arrived, gain = fence((partner(given), gain))
    stream = swapped(call(stream_kernel, chunk, (kept, arrived), [NEAR] * 2))
    part = shaped((half_tokens, half_width), jnp.bfloat16)
    own, other = call(norm_kernel, (part, part), (stream, gain), [NEAR] * 2)
    step = block_of(half_width, 512)
    mine = call(
        head_kernel,
        shaped((tokens, columns_here + 1), jnp.float32),
        (own, partner(other), targets, head_weight.T),
        [NEAR, NEAR, NEAR, FAR],
        [
            VECTOR((columns_here, half_width), jnp.bfloat16),
            VECTOR((tokens, half_width), jnp.bfloat16),
            DMA((half_width // step,)),
        ],
        grant=12 << 20,
    )
    row = shaped((vocab_count, 1, 3 * tokens), jnp.float32)
    stats = call(stats_kernel, row, (mine, partner(mine)), [NEAR] * 2)
    model_count = lax.axis_size("mp")
    mixed = [
        [peer * model_count + (peer + core) % model_count for peer in range(vocab_count)]
        for core in range(model_count)
    ]
    stats, is_low = fence((stats, lax.axis_index("mp") == 0))
    stats = fence(
        lax.all_to_all(stats, ("vocab", "mp"), 0, 0, tiled=True, axis_index_groups=mixed)
    )
    tops, totals, chosen = jnp.split(stats[:, 0], 3, axis=1)
    top = jnp.max(tops, axis=0)
    total = jnp.sum(totals * jnp.exp(tops - top[None]), axis=0)
    chosen = jnp.sum(chosen, axis=0)
    low, high = (
        tuple(one[side] for one in (top, total, chosen))
        for side in (slice(None, half_tokens), slice(half_tokens, None))
    )
    top, total, chosen = (jnp.where(is_low, here, there) for here, there in zip(low, high))
    return chosen - top - jnp.log(total)


def solution(mesh):
    return jax.shard_map(
        body,
        mesh=mesh,
        in_specs=(
            P(("groups", "vocab"), "mp"),
            P(("groups", "vocab"), "mp"),
            P("vocab", "mp"),
            P(("groups", "vocab", "mp"), None),
            P(),
            P("mp", "vocab"),
            P(("groups", "mp")),
        ),
        out_specs=P(("groups", "mp")),
        check_vma=False,
    )
```

```python
import jax
import jax.numpy as jnp
from jax import lax
from jax.experimental import pallas as pl
from jax.experimental.pallas import tpu as pltpu
from jax.sharding import PartitionSpec as P

EPSILON = 1e-05
ROWS_BY_ROWS = (((1,), (1,)), ((), ()))
SMALL = 2 << 20
HEAD_STEP = 1024
fence = lax.optimization_barrier
NEAR = pl.BlockSpec(memory_space=pltpu.VMEM)
FAR = pl.BlockSpec(memory_space=pltpu.HBM)
VECTOR = pltpu.VMEM
DMA = pltpu.SemaphoreType.DMA


def partner(value):
    return lax.ppermute(value, "mp", [(0, 1), (1, 0)])


def swapped(value):
    return fence(lax.all_to_all(fence(value), "vocab", 0, 0, tiled=True))


def fetched(weight, first, size):
    def kernel(weight_hbm, out_ref, done):
        load = pltpu.make_async_copy(weight_hbm.at[:, pl.ds(first, size)], out_ref, done)
        load.start()
        load.wait()

    rows = weight.shape[0]
    return pl.pallas_call(
        kernel,
        out_shape=pltpu.VMEM((rows, size), weight.dtype),
        in_specs=[FAR],
        out_specs=pl.BlockSpec(memory_space=pl.ANY),
        scratch_shapes=[DMA],
        cost_estimate=pl.CostEstimate(flops=0, bytes_accessed=4 * rows * size, transcendentals=0),
        compiler_params=pltpu.CompilerParams(vmem_limit_bytes=SMALL),
    )(pltpu.with_memory_space_constraint(weight, pltpu.HBM))


def call(kernel, out_shape, operands, places, scratch=(), grant=SMALL):
    operands = tuple(
        pltpu.with_memory_space_constraint(one, pltpu.HBM) if place is FAR else one
        for one, place in zip(operands, places)
    )
    return pl.pallas_call(
        kernel,
        out_shape=out_shape,
        in_specs=places,
        out_specs=jax.tree.map(lambda _: NEAR, out_shape),
        scratch_shapes=list(scratch),
        compiler_params=pltpu.CompilerParams(vmem_limit_bytes=grant),
    )(*operands)


def block_of(length, most):
    return max(size for size in range(1, most + 1) if length % size == 0)


def gated_kernel(gate_hbm, up_hbm, residual_hbm, out_ref, gate_ref, up_ref, residual_ref, done):
    loads = (
        pltpu.make_async_copy(gate_hbm, gate_ref, done.at[0]),
        pltpu.make_async_copy(up_hbm, up_ref, done.at[1]),
        pltpu.make_async_copy(residual_hbm, residual_ref, done.at[2]),
    )
    for load in loads:
        load.start()
    for load in loads:
        load.wait()
    count, rows, width = out_ref.shape
    units = gate_ref.shape[1]
    extra = width - units
    gate = gate_ref[...].astype(jnp.float32)
    up = up_ref[...].astype(jnp.float32)
    gated = (gate / (1.0 + jnp.exp(-gate)) * up).astype(jnp.bfloat16)
    for peer in range(count):
        out_ref[peer, :, :units] = gated
        for row in range(rows):
            first = (peer * rows + row) * extra
            out_ref[peer, row : row + 1, units:] = residual_ref[:, first : first + extra]


def weight_loads(weight_hbm, weight_ref, done):
    depth = weight_ref.shape[1] // done.shape[0]
    first = weight_hbm.shape[1] - weight_ref.shape[1]
    loads = []
    for part in range(done.shape[0]):
        loads.append(
            pltpu.make_async_copy(
                weight_hbm.at[:, pl.ds(first + part * depth, depth)],
                weight_ref.at[:, pl.ds(part * depth, depth)],
                done.at[part],
            )
        )
        loads[-1].start()
    return loads


def product(terms, left_ref, early, weight_ref, loads):
    depth = weight_ref.shape[1] // len(loads)
    at = 0
    for here in early:
        terms += lax.dot_general(
            left_ref[:, at : at + here.shape[1]],
            here[...],
            ROWS_BY_ROWS,
            preferred_element_type=jnp.float32,
        )
        at += here.shape[1]
    for part, load in enumerate(loads):
        load.wait()
        terms += lax.dot_general(
            left_ref[:, at : at + depth],
            weight_ref[:, part * depth : (part + 1) * depth],
            ROWS_BY_ROWS,
            preferred_element_type=jnp.float32,
        )
        at += depth
    return terms


def down_kernel(chunks_ref, weight_hbm, kept_ref, given_ref, weight_ref, units_ref, own_ref, done):
    loads = weight_loads(weight_hbm, weight_ref, done)
    units = weight_hbm.shape[1]
    count, rows, width = chunks_ref.shape
    half, block = kept_ref.shape
    index = lax.axis_index("mp")
    token = lax.broadcasted_iota(jnp.int32, (rows, block), 0)
    for peer in range(count):
        units_ref[peer * rows : (peer + 1) * rows, :] = chunks_ref[peer, :, :units]
        pieces = [chunks_ref[peer, row : row + 1, units:].astype(jnp.float32) for row in range(rows)]
        residual = jnp.broadcast_to(jnp.concatenate(pieces, axis=1), (rows, block))
        own_ref[peer * rows : (peer + 1) * rows, :] = jnp.where(token == index, residual, 0.0)
    terms = product(own_ref[...], units_ref, (), weight_ref, loads)
    low, high = terms[:half], terms[half:]
    kept_ref[...] = jnp.where(index == 0, low, high)
    given_ref[...] = jnp.where(index == 0, high, low)


def stream_kernel(kept_ref, arrived_ref, out_ref):
    stream = (kept_ref[...] + arrived_ref[...]).astype(jnp.bfloat16)
    for peer in range(out_ref.shape[0]):
        out_ref[peer] = stream


def norm_kernel(stream_ref, gain_ref, own_ref, other_ref):
    count, tokens, block = stream_ref.shape
    half = count // 2
    squares = jnp.zeros((tokens, block), jnp.float32)
    for part in range(count):
        values = stream_ref[part].astype(jnp.float32)
        squares += values * values
    mean_square = jnp.sum(squares, axis=1, keepdims=True) / (count * block)
    scale = lax.rsqrt(mean_square + EPSILON)
    index = lax.axis_index("mp")
    for out_ref, side in ((own_ref, index), (other_ref, 1 - index)):
        for part in range(half):
            at = side * half + part
            gain = gain_ref[pl.ds(at, 1), :]
            values = stream_ref[at].astype(jnp.float32) * scale * gain
            out_ref[:, part * block : (part + 1) * block] = values.astype(jnp.bfloat16)


def column_of(row_ref):
    size = row_ref.shape[0]
    square = (size, size)
    diagonal = lax.broadcasted_iota(jnp.int32, square, 0) == lax.broadcasted_iota(
        jnp.int32, square, 1
    )
    spread = jnp.broadcast_to(row_ref[...].reshape(1, size), square).astype(jnp.float32)
    return jnp.sum(jnp.where(diagonal, spread, 0.0), axis=1, keepdims=True)


def head_kernel(own_ref, other_ref, targets_ref, *refs):
    *early, weight_hbm, out_ref, weight_ref, halves_ref, done = refs
    loads = weight_loads(weight_hbm, weight_ref, done)
    tokens = own_ref.shape[0]
    columns = weight_ref.shape[0]
    halves_ref[...] = jnp.concatenate([own_ref[...], other_ref[...]], axis=0)
    out_ref[:tokens, columns:] = column_of(targets_ref)
    out_ref[tokens:, columns:] = jnp.zeros((tokens, 1), jnp.float32)
    terms = jnp.zeros((2 * tokens, columns), jnp.float32)
    out_ref[:, :columns] = product(terms, halves_ref, early, weight_ref, loads)


def stats_kernel(mine_ref, arrived_ref, out_ref):
    half = mine_ref.shape[0] // 2
    columns = mine_ref.shape[1] - 1
    own = mine_ref[:half, :] + arrived_ref[half:, :]
    other = mine_ref[half:, :] + arrived_ref[:half, :]
    is_low = lax.axis_index("mp") == 0
    both = jnp.concatenate(
        [jnp.where(is_low, own, other), jnp.where(is_low, other, own)], axis=0
    )
    logits, wanted = both[:, :columns], both[:, columns:].astype(jnp.int32)
    tokens = 2 * half
    wanted -= lax.axis_index("vocab") * columns
    here = lax.broadcasted_iota(jnp.int32, logits.shape, 1) == wanted
    chosen = jnp.sum(jnp.where(here, logits, 0.0), axis=1, keepdims=True)
    top = jnp.max(logits, axis=1, keepdims=True)
    total = jnp.sum(jnp.exp(logits - top), axis=1, keepdims=True)
    lane = lax.broadcasted_iota(jnp.int32, (tokens, 3 * tokens), 1)
    token = lax.broadcasted_iota(jnp.int32, (tokens, 3 * tokens), 0)
    row = jnp.zeros((tokens, 3 * tokens), jnp.float32)
    for place, value in enumerate((top, total, chosen)):
        row = jnp.where(lane == token + place * tokens, value, row)
    row = jnp.sum(row, axis=0, keepdims=True)
    for peer in range(out_ref.shape[0]):
        out_ref[peer] = row


def body(gate_pre, up_pre, down_weight, residual, norm_gain, head_weight, targets):
    vocab_count = lax.axis_size("vocab")
    rows, half_units = gate_pre.shape
    block = down_weight.shape[0]
    tokens = rows * vocab_count
    half_tokens = targets.shape[0]
    half_width, columns_here = head_weight.shape
    shaped = jax.ShapeDtypeStruct
    step = block_of(half_units, 512)
    extra = residual.shape[0] * block // rows
    chunk = shaped((vocab_count, rows, half_units + extra), jnp.bfloat16)
    operands = (gate_pre, up_pre, residual)
    places = [VECTOR(one.shape, one.dtype) for one in operands]
    chunks = swapped(call(gated_kernel, chunk, operands, [FAR] * 3, places + [DMA((3,))]))
    part = shaped((half_tokens, block), jnp.float32)
    kept, given = call(
        down_kernel,
        (part, part),
        (chunks, down_weight),
        [NEAR, FAR],
        [
            VECTOR(down_weight.shape, jnp.bfloat16),
            VECTOR((tokens, half_units), jnp.bfloat16),
            VECTOR((tokens, block), jnp.float32),
            DMA((half_units // step,)),
        ],
        grant=24 << 20,
    )
    step = block_of(half_width, HEAD_STEP)
    given, head_rows = fence((given, head_weight.T))
    first = fetched(head_rows, 0, step)
    chunk = shaped((vocab_count, half_tokens, block), jnp.bfloat16)
    gain = norm_gain.astype(jnp.float32).reshape(vocab_count, block)
    arrived, gain, first = fence((partner(given), gain, first))
    stream = swapped(call(stream_kernel, chunk, (kept, arrived), [NEAR] * 2))
    part = shaped((half_tokens, half_width), jnp.bfloat16)
    own, other = call(norm_kernel, (part, part), (stream, gain), [NEAR] * 2)
    other, head_rows = fence((other, head_rows))
    early = (first, fetched(head_rows, step, step))
    rest = half_width - 2 * step
    mine = call(
        head_kernel,
        shaped((tokens, columns_here + 1), jnp.float32),
        (own, partner(other), targets, *early, head_rows),
        [NEAR] * 5 + [FAR],
        [
            VECTOR((columns_here, rest), jnp.bfloat16),
            VECTOR((tokens, half_width), jnp.bfloat16),
            DMA((rest // block_of(rest, 512),)),
        ],
        grant=12 << 20,
    )
    row = shaped((vocab_count, 1, 3 * tokens), jnp.float32)
    stats = call(stats_kernel, row, (mine, partner(mine)), [NEAR] * 2)
    model_count = lax.axis_size("mp")
    mixed = [
        [peer * model_count + (peer + core) % model_count for peer in range(vocab_count)]
        for core in range(model_count)
    ]
    stats, is_low = fence((stats, lax.axis_index("mp") == 0))
    stats = fence(
        lax.all_to_all(stats, ("vocab", "mp"), 0, 0, tiled=True, axis_index_groups=mixed)
    )
    tops, totals, chosen = jnp.split(stats[:, 0], 3, axis=1)
    top = jnp.max(tops, axis=0)
    total = jnp.sum(totals * jnp.exp(tops - top[None]), axis=0)
    chosen = jnp.sum(chosen, axis=0)
    low, high = (
        tuple(one[side] for one in (top, total, chosen))
        for side in (slice(None, half_tokens), slice(half_tokens, None))
    )
    top, total, chosen = (jnp.where(is_low, here, there) for here, there in zip(low, high))
    return chosen - top - jnp.log(total)


def solution(mesh):
    return jax.shard_map(
        body,
        mesh=mesh,
        in_specs=(
            P(("groups", "vocab"), "mp"),
            P(("groups", "vocab"), "mp"),
            P("vocab", "mp"),
            P(("groups", "vocab", "mp"), None),
            P(),
            P("mp", "vocab"),
            P(("groups", "mp")),
        ),
        out_specs=P(("groups", "mp")),
        check_vma=False,
    )
```

```python
import jax
import jax.numpy as jnp
from jax import lax
from jax.experimental import pallas as pl
from jax.experimental.pallas import tpu as pltpu
from jax.sharding import PartitionSpec as P

EPSILON = 1e-05
ROWS_BY_ROWS = (((1,), (1,)), ((), ()))
SMALL = 2 << 20
EARLY = 3
fence = lax.optimization_barrier
NEAR = pl.BlockSpec(memory_space=pltpu.VMEM)
FAR = pl.BlockSpec(memory_space=pltpu.HBM)
VECTOR = pltpu.VMEM
DMA = pltpu.SemaphoreType.DMA


def partner(value):
    return lax.ppermute(value, "mp", [(0, 1), (1, 0)])


def swapped(value):
    return fence(lax.all_to_all(fence(value), "vocab", 0, 0, tiled=True))


def fetched(weight, first, size):
    def kernel(weight_hbm, out_ref, done):
        load = pltpu.make_async_copy(weight_hbm.at[:, pl.ds(first, size)], out_ref, done)
        load.start()
        load.wait()

    rows = weight.shape[0]
    return pl.pallas_call(
        kernel,
        out_shape=pltpu.VMEM((rows, size), weight.dtype),
        in_specs=[FAR],
        out_specs=pl.BlockSpec(memory_space=pl.ANY),
        scratch_shapes=[DMA],
        cost_estimate=pl.CostEstimate(flops=0, bytes_accessed=4 * rows * size, transcendentals=0),
        compiler_params=pltpu.CompilerParams(vmem_limit_bytes=SMALL),
    )(pltpu.with_memory_space_constraint(weight, pltpu.HBM))


def call(kernel, out_shape, operands, places, scratch=(), grant=SMALL):
    operands = tuple(
        pltpu.with_memory_space_constraint(one, pltpu.HBM) if place is FAR else one
        for one, place in zip(operands, places)
    )
    return pl.pallas_call(
        kernel,
        out_shape=out_shape,
        in_specs=places,
        out_specs=jax.tree.map(lambda _: NEAR, out_shape),
        scratch_shapes=list(scratch),
        compiler_params=pltpu.CompilerParams(vmem_limit_bytes=grant),
    )(*operands)


def block_of(length, most):
    return max(size for size in range(1, most + 1) if length % size == 0)


def gated_kernel(gate_hbm, up_hbm, residual_hbm, out_ref, gate_ref, up_ref, residual_ref, done):
    loads = (
        pltpu.make_async_copy(gate_hbm, gate_ref, done.at[0]),
        pltpu.make_async_copy(up_hbm, up_ref, done.at[1]),
        pltpu.make_async_copy(residual_hbm, residual_ref, done.at[2]),
    )
    for load in loads:
        load.start()
    for load in loads:
        load.wait()
    count, rows, width = out_ref.shape
    units = gate_ref.shape[1]
    extra = width - units
    gate = gate_ref[...].astype(jnp.float32)
    up = up_ref[...].astype(jnp.float32)
    gated = (gate / (1.0 + jnp.exp(-gate)) * up).astype(jnp.bfloat16)
    for peer in range(count):
        out_ref[peer, :, :units] = gated
        for row in range(rows):
            first = (peer * rows + row) * extra
            out_ref[peer, row : row + 1, units:] = residual_ref[:, first : first + extra]


def weight_loads(weight_hbm, weight_ref, done):
    depth = weight_ref.shape[1] // done.shape[0]
    first = weight_hbm.shape[1] - weight_ref.shape[1]
    loads = []
    for part in range(done.shape[0]):
        loads.append(
            pltpu.make_async_copy(
                weight_hbm.at[:, pl.ds(first + part * depth, depth)],
                weight_ref.at[:, pl.ds(part * depth, depth)],
                done.at[part],
            )
        )
        loads[-1].start()
    return loads


def product(terms, left_ref, early, weight_ref, loads):
    depth = weight_ref.shape[1] // len(loads)
    at = 0
    for here in early:
        terms += lax.dot_general(
            left_ref[:, at : at + here.shape[1]],
            here[...],
            ROWS_BY_ROWS,
            preferred_element_type=jnp.float32,
        )
        at += here.shape[1]
    for part, load in enumerate(loads):
        load.wait()
        terms += lax.dot_general(
            left_ref[:, at : at + depth],
            weight_ref[:, part * depth : (part + 1) * depth],
            ROWS_BY_ROWS,
            preferred_element_type=jnp.float32,
        )
        at += depth
    return terms


def down_kernel(
    chunks_ref, early_ref, weight_hbm, kept_ref, given_ref, weight_ref, units_ref, own_ref, done
):
    loads = weight_loads(weight_hbm, weight_ref, done)
    units = weight_hbm.shape[1]
    count, rows, width = chunks_ref.shape
    half, block = kept_ref.shape
    index = lax.axis_index("mp")
    token = lax.broadcasted_iota(jnp.int32, (rows, block), 0)
    for peer in range(count):
        units_ref[peer * rows : (peer + 1) * rows, :] = chunks_ref[peer, :, :units]
        pieces = [chunks_ref[peer, row : row + 1, units:].astype(jnp.float32) for row in range(rows)]
        residual = jnp.broadcast_to(jnp.concatenate(pieces, axis=1), (rows, block))
        own_ref[peer * rows : (peer + 1) * rows, :] = jnp.where(token == index, residual, 0.0)
    terms = product(own_ref[...], units_ref, (early_ref,), weight_ref, loads)
    low, high = terms[:half], terms[half:]
    kept_ref[...] = jnp.where(index == 0, low, high)
    given_ref[...] = jnp.where(index == 0, high, low)


def stream_kernel(kept_ref, arrived_ref, out_ref):
    stream = (kept_ref[...] + arrived_ref[...]).astype(jnp.bfloat16)
    for peer in range(out_ref.shape[0]):
        out_ref[peer] = stream


def norm_kernel(stream_ref, gain_ref, own_ref, other_ref):
    count, tokens, block = stream_ref.shape
    half = count // 2
    squares = jnp.zeros((tokens, block), jnp.float32)
    for part in range(count):
        values = stream_ref[part].astype(jnp.float32)
        squares += values * values
    mean_square = jnp.sum(squares, axis=1, keepdims=True) / (count * block)
    scale = lax.rsqrt(mean_square + EPSILON)
    index = lax.axis_index("mp")
    for out_ref, side in ((own_ref, index), (other_ref, 1 - index)):
        for part in range(half):
            at = side * half + part
            gain = gain_ref[pl.ds(at, 1), :]
            values = stream_ref[at].astype(jnp.float32) * scale * gain
            out_ref[:, part * block : (part + 1) * block] = values.astype(jnp.bfloat16)


def column_of(row_ref):
    size = row_ref.shape[0]
    square = (size, size)
    diagonal = lax.broadcasted_iota(jnp.int32, square, 0) == lax.broadcasted_iota(
        jnp.int32, square, 1
    )
    spread = jnp.broadcast_to(row_ref[...].reshape(1, size), square).astype(jnp.float32)
    return jnp.sum(jnp.where(diagonal, spread, 0.0), axis=1, keepdims=True)


def head_kernel(own_ref, other_ref, targets_ref, *refs):
    *early, weight_hbm, out_ref, weight_ref, halves_ref, done = refs
    loads = weight_loads(weight_hbm, weight_ref, done)
    tokens = own_ref.shape[0]
    columns = weight_ref.shape[0]
    halves_ref[...] = jnp.concatenate([own_ref[...], other_ref[...]], axis=0)
    out_ref[:tokens, columns:] = column_of(targets_ref)
    out_ref[tokens:, columns:] = jnp.zeros((tokens, 1), jnp.float32)
    terms = jnp.zeros((2 * tokens, columns), jnp.float32)
    out_ref[:, :columns] = product(terms, halves_ref, early, weight_ref, loads)


def stats_kernel(mine_ref, arrived_ref, out_ref):
    half = mine_ref.shape[0] // 2
    columns = mine_ref.shape[1] - 1
    own = mine_ref[:half, :] + arrived_ref[half:, :]
    other = mine_ref[half:, :] + arrived_ref[:half, :]
    is_low = lax.axis_index("mp") == 0
    both = jnp.concatenate(
        [jnp.where(is_low, own, other), jnp.where(is_low, other, own)], axis=0
    )
    logits, wanted = both[:, :columns], both[:, columns:].astype(jnp.int32)
    tokens = 2 * half
    wanted -= lax.axis_index("vocab") * columns
    here = lax.broadcasted_iota(jnp.int32, logits.shape, 1) == wanted
    chosen = jnp.sum(jnp.where(here, logits, 0.0), axis=1, keepdims=True)
    top = jnp.max(logits, axis=1, keepdims=True)
    total = jnp.sum(jnp.exp(logits - top), axis=1, keepdims=True)
    lane = lax.broadcasted_iota(jnp.int32, (tokens, 3 * tokens), 1)
    token = lax.broadcasted_iota(jnp.int32, (tokens, 3 * tokens), 0)
    row = jnp.zeros((tokens, 3 * tokens), jnp.float32)
    for place, value in enumerate((top, total, chosen)):
        row = jnp.where(lane == token + place * tokens, value, row)
    row = jnp.sum(row, axis=0, keepdims=True)
    for peer in range(out_ref.shape[0]):
        out_ref[peer] = row


def body(gate_pre, up_pre, down_weight, residual, norm_gain, head_weight, targets):
    vocab_count = lax.axis_size("vocab")
    rows, half_units = gate_pre.shape
    block = down_weight.shape[0]
    tokens = rows * vocab_count
    half_tokens = targets.shape[0]
    half_width, columns_here = head_weight.shape
    shaped = jax.ShapeDtypeStruct
    step = block_of(half_units, 512)
    extra = residual.shape[0] * block // rows
    chunk = shaped((vocab_count, rows, half_units + extra), jnp.bfloat16)
    operands = (gate_pre, up_pre, residual)
    places = [VECTOR(one.shape, one.dtype) for one in operands]
    chunks = call(gated_kernel, chunk, operands, [FAR] * 3, places + [DMA((3,))])
    chunks, down_weight = fence((chunks, down_weight))
    early = fetched(down_weight, 0, EARLY * step)
    chunks = lax.all_to_all(chunks, "vocab", 0, 0, tiled=True)
    chunks, early = fence((chunks, early))
    rest = half_units - EARLY * step
    part = shaped((half_tokens, block), jnp.float32)
    kept, given = call(
        down_kernel,
        (part, part),
        (chunks, early, down_weight),
        [NEAR, NEAR, FAR],
        [
            VECTOR((block, rest), jnp.bfloat16),
            VECTOR((tokens, half_units), jnp.bfloat16),
            VECTOR((tokens, block), jnp.float32),
            DMA((rest // step,)),
        ],
        grant=24 << 20,
    )
    chunk = shaped((vocab_count, half_tokens, block), jnp.bfloat16)
    gain = norm_gain.astype(jnp.float32).reshape(vocab_count, block)
    arrived, gain = fence((partner(given), gain))
    stream = swapped(call(stream_kernel, chunk, (kept, arrived), [NEAR] * 2))
    part = shaped((half_tokens, half_width), jnp.bfloat16)
    own, other = call(norm_kernel, (part, part), (stream, gain), [NEAR] * 2)
    mine = call(
        head_kernel,
        shaped((tokens, columns_here + 1), jnp.float32),
        (own, partner(other), targets, head_weight.T),
        [NEAR] * 3 + [FAR],
        [
            VECTOR((columns_here, half_width), jnp.bfloat16),
            VECTOR((tokens, half_width), jnp.bfloat16),
            DMA((half_width // block_of(half_width, 512),)),
        ],
        grant=12 << 20,
    )
    row = shaped((vocab_count, 1, 3 * tokens), jnp.float32)
    stats = call(stats_kernel, row, (mine, partner(mine)), [NEAR] * 2)
    model_count = lax.axis_size("mp")
    mixed = [
        [peer * model_count + (peer + core) % model_count for peer in range(vocab_count)]
        for core in range(model_count)
    ]
    stats, is_low = fence((stats, lax.axis_index("mp") == 0))
    stats = fence(
        lax.all_to_all(stats, ("vocab", "mp"), 0, 0, tiled=True, axis_index_groups=mixed)
    )
    tops, totals, chosen = jnp.split(stats[:, 0], 3, axis=1)
    top = jnp.max(tops, axis=0)
    total = jnp.sum(totals * jnp.exp(tops - top[None]), axis=0)
    chosen = jnp.sum(chosen, axis=0)
    low, high = (
        tuple(one[side] for one in (top, total, chosen))
        for side in (slice(None, half_tokens), slice(half_tokens, None))
    )
    top, total, chosen = (jnp.where(is_low, here, there) for here, there in zip(low, high))
    return chosen - top - jnp.log(total)


def solution(mesh):
    return jax.shard_map(
        body,
        mesh=mesh,
        in_specs=(
            P(("groups", "vocab"), "mp"),
            P(("groups", "vocab"), "mp"),
            P("vocab", "mp"),
            P(("groups", "vocab", "mp"), None),
            P(),
            P("mp", "vocab"),
            P(("groups", "mp")),
        ),
        out_specs=P(("groups", "mp")),
        check_vma=False,
    )
```

```python
import jax
import jax.numpy as jnp
from jax import lax
from jax.experimental import pallas as pl
from jax.experimental.pallas import tpu as pltpu
from jax.sharding import PartitionSpec as P

EPSILON = 1e-05
ROWS_BY_ROWS = (((1,), (1,)), ((), ()))
SMALL = 2 << 20
EARLY = 3
CHUNKS_GRANT = 8 << 20
fence = lax.optimization_barrier
NEAR = pl.BlockSpec(memory_space=pltpu.VMEM)
FAR = pl.BlockSpec(memory_space=pltpu.HBM)
FREE = pl.BlockSpec(memory_space=pl.ANY)
VECTOR = pltpu.VMEM
DMA = pltpu.SemaphoreType.DMA


def partner(value):
    return lax.ppermute(value, "mp", [(0, 1), (1, 0)])


def fetched(weight, sizes):
    def kernel(weight_hbm, *refs):
        *outs, done = refs
        loads, first = [], 0
        for out_ref in outs:
            here = pl.ds(first, out_ref.shape[1])
            loads.append(
                pltpu.make_async_copy(weight_hbm.at[:, here], out_ref, done.at[len(loads)])
            )
            loads[-1].start()
            first += out_ref.shape[1]
        for load in loads:
            load.wait()

    rows = weight.shape[0]
    return pl.pallas_call(
        kernel,
        out_shape=tuple(pltpu.VMEM((rows, size), weight.dtype) for size in sizes),
        in_specs=[FAR],
        out_specs=(FREE,) * len(sizes),
        scratch_shapes=[DMA((len(sizes),))],
        cost_estimate=pl.CostEstimate(
            flops=0, bytes_accessed=4 * rows * sum(sizes), transcendentals=0
        ),
        compiler_params=pltpu.CompilerParams(vmem_limit_bytes=SMALL),
    )(pltpu.with_memory_space_constraint(weight, pltpu.HBM))


def call(kernel, out_shape, operands, places, scratch=(), grant=SMALL, results=None):
    operands = tuple(
        pltpu.with_memory_space_constraint(one, pltpu.HBM) if place is FAR else one
        for one, place in zip(operands, places)
    )
    return pl.pallas_call(
        kernel,
        out_shape=out_shape,
        in_specs=places,
        out_specs=results or jax.tree.map(lambda _: NEAR, out_shape),
        scratch_shapes=list(scratch),
        compiler_params=pltpu.CompilerParams(vmem_limit_bytes=grant),
    )(*operands)


def block_of(length, most):
    return max(size for size in range(1, most + 1) if length % size == 0)


def gated_kernel(
    gate_hbm, up_hbm, residual_hbm, out_hbm, gate_ref, up_ref, residual_ref, out_ref, done, sent
):
    loads = (
        pltpu.make_async_copy(gate_hbm, gate_ref, done.at[0]),
        pltpu.make_async_copy(up_hbm, up_ref, done.at[1]),
        pltpu.make_async_copy(residual_hbm, residual_ref, done.at[2]),
    )
    for load in loads:
        load.start()
    for load in loads:
        load.wait()
    count, rows, width = out_ref.shape
    units = gate_ref.shape[1]
    extra = width - units
    gate = gate_ref[...].astype(jnp.float32)
    up = up_ref[...].astype(jnp.float32)
    gated = (gate / (1.0 + jnp.exp(-gate)) * up).astype(jnp.bfloat16)
    stores = []
    for peer in range(count):
        out_ref[peer, :, :units] = gated
        for row in range(rows):
            first = (peer * rows + row) * extra
            out_ref[peer, row : row + 1, units:] = residual_ref[:, first : first + extra]
        stores.append(pltpu.make_async_copy(out_ref.at[peer], out_hbm.at[peer], sent.at[peer]))
        stores[-1].start()
    for store in stores:
        store.wait()


def weight_loads(weight_hbm, weight_ref, done):
    depth = weight_ref.shape[1] // done.shape[0]
    first = weight_hbm.shape[1] - weight_ref.shape[1]
    loads = []
    for part in range(done.shape[0]):
        loads.append(
            pltpu.make_async_copy(
                weight_hbm.at[:, pl.ds(first + part * depth, depth)],
                weight_ref.at[:, pl.ds(part * depth, depth)],
                done.at[part],
            )
        )
        loads[-1].start()
    return loads


def product(terms, left_ref, early, weight_ref, loads):
    depth = weight_ref.shape[1] // len(loads)
    at = 0
    for here in early:
        terms += lax.dot_general(
            left_ref[:, at : at + here.shape[1]],
            here[...],
            ROWS_BY_ROWS,
            preferred_element_type=jnp.float32,
        )
        at += here.shape[1]
    for part, load in enumerate(loads):
        load.wait()
        terms += lax.dot_general(
            left_ref[:, at : at + depth],
            weight_ref[:, part * depth : (part + 1) * depth],
            ROWS_BY_ROWS,
            preferred_element_type=jnp.float32,
        )
        at += depth
    return terms


def down_kernel(
    chunks_ref, early_ref, weight_hbm, kept_ref, given_ref, weight_ref, units_ref, own_ref, done
):
    loads = weight_loads(weight_hbm, weight_ref, done)
    units = weight_hbm.shape[1]
    count, rows, width = chunks_ref.shape
    half, block = kept_ref.shape
    index = lax.axis_index("mp")
    token = lax.broadcasted_iota(jnp.int32, (rows, block), 0)
    for peer in range(count):
        units_ref[peer * rows : (peer + 1) * rows, :] = chunks_ref[peer, :, :units]
        pieces = [chunks_ref[peer, row : row + 1, units:].astype(jnp.float32) for row in range(rows)]
        residual = jnp.broadcast_to(jnp.concatenate(pieces, axis=1), (rows, block))
        own_ref[peer * rows : (peer + 1) * rows, :] = jnp.where(token == index, residual, 0.0)
    terms = product(own_ref[...], units_ref, (early_ref,), weight_ref, loads)
    low, high = terms[:half], terms[half:]
    kept_ref[...] = jnp.where(index == 0, low, high)
    given_ref[...] = jnp.where(index == 0, high, low)


def stream_kernel(kept_ref, arrived_ref, out_hbm, stream_ref, sent):
    stream_ref[...] = (kept_ref[...] + arrived_ref[...]).astype(jnp.bfloat16)
    stores = [
        pltpu.make_async_copy(stream_ref, out_hbm.at[peer], sent.at[peer])
        for peer in range(out_hbm.shape[0])
    ]
    for store in stores:
        store.start()
    for store in stores:
        store.wait()


def norm_kernel(stream_ref, gain_ref, own_ref, other_ref):
    count, tokens, block = stream_ref.shape
    half = count // 2
    squares = jnp.zeros((tokens, block), jnp.float32)
    for part in range(count):
        values = stream_ref[part].astype(jnp.float32)
        squares += values * values
    mean_square = jnp.sum(squares, axis=1, keepdims=True) / (count * block)
    scale = lax.rsqrt(mean_square + EPSILON)
    index = lax.axis_index("mp")
    for out_ref, side in ((own_ref, index), (other_ref, 1 - index)):
        for part in range(half):
            at = side * half + part
            gain = gain_ref[pl.ds(at, 1), :]
            values = stream_ref[at].astype(jnp.float32) * scale * gain
            out_ref[:, part * block : (part + 1) * block] = values.astype(jnp.bfloat16)


def column_of(row_ref):
    size = row_ref.shape[0]
    square = (size, size)
    diagonal = lax.broadcasted_iota(jnp.int32, square, 0) == lax.broadcasted_iota(
        jnp.int32, square, 1
    )
    spread = jnp.broadcast_to(row_ref[...].reshape(1, size), square).astype(jnp.float32)
    return jnp.sum(jnp.where(diagonal, spread, 0.0), axis=1, keepdims=True)


def head_kernel(own_ref, other_ref, targets_ref, *refs):
    *early, weight_hbm, out_ref, weight_ref, halves_ref, done = refs
    loads = weight_loads(weight_hbm, weight_ref, done)
    tokens = own_ref.shape[0]
    columns = weight_ref.shape[0]
    halves_ref[...] = jnp.concatenate([own_ref[...], other_ref[...]], axis=0)
    out_ref[:tokens, columns:] = column_of(targets_ref)
    out_ref[tokens:, columns:] = jnp.zeros((tokens, 1), jnp.float32)
    terms = jnp.zeros((2 * tokens, columns), jnp.float32)
    out_ref[:, :columns] = product(terms, halves_ref, early, weight_ref, loads)


def stats_kernel(mine_ref, arrived_ref, out_ref):
    half = mine_ref.shape[0] // 2
    columns = mine_ref.shape[1] - 1
    own = mine_ref[:half, :] + arrived_ref[half:, :]
    other = mine_ref[half:, :] + arrived_ref[:half, :]
    is_low = lax.axis_index("mp") == 0
    both = jnp.concatenate(
        [jnp.where(is_low, own, other), jnp.where(is_low, other, own)], axis=0
    )
    logits, wanted = both[:, :columns], both[:, columns:].astype(jnp.int32)
    tokens = 2 * half
    wanted -= lax.axis_index("vocab") * columns
    here = lax.broadcasted_iota(jnp.int32, logits.shape, 1) == wanted
    chosen = jnp.sum(jnp.where(here, logits, 0.0), axis=1, keepdims=True)
    top = jnp.max(logits, axis=1, keepdims=True)
    total = jnp.sum(jnp.exp(logits - top), axis=1, keepdims=True)
    lane = lax.broadcasted_iota(jnp.int32, (tokens, 3 * tokens), 1)
    token = lax.broadcasted_iota(jnp.int32, (tokens, 3 * tokens), 0)
    row = jnp.zeros((tokens, 3 * tokens), jnp.float32)
    for place, value in enumerate((top, total, chosen)):
        row = jnp.where(lane == token + place * tokens, value, row)
    row = jnp.sum(row, axis=0, keepdims=True)
    for peer in range(out_ref.shape[0]):
        out_ref[peer] = row


def body(gate_pre, up_pre, down_weight, residual, norm_gain, head_weight, targets):
    vocab_count = lax.axis_size("vocab")
    rows, half_units = gate_pre.shape
    block = down_weight.shape[0]
    tokens = rows * vocab_count
    half_tokens = targets.shape[0]
    half_width, columns_here = head_weight.shape
    shaped = jax.ShapeDtypeStruct
    step = block_of(half_units, 512)
    extra = residual.shape[0] * block // rows
    chunk = shaped((vocab_count, rows, half_units + extra), jnp.bfloat16)
    operands = (gate_pre, up_pre, residual)
    places = [VECTOR(one.shape, one.dtype) for one in operands]
    places += [VECTOR(chunk.shape, chunk.dtype), DMA((3,)), DMA((vocab_count,))]
    chunks = call(
        gated_kernel, chunk, operands, [FAR] * 3, places, CHUNKS_GRANT, FREE
    )
    chunks, down_weight = fence((chunks, down_weight))
    (early,) = fetched(down_weight, (EARLY * step,))
    chunks = lax.all_to_all(chunks, "vocab", 0, 0, tiled=True)
    chunks, early = fence((chunks, early))
    rest = half_units - EARLY * step
    part = shaped((half_tokens, block), jnp.float32)
    kept, given = call(
        down_kernel,
        (part, part),
        (chunks, early, down_weight),
        [NEAR, NEAR, FAR],
        [
            VECTOR((block, rest), jnp.bfloat16),
            VECTOR((tokens, half_units), jnp.bfloat16),
            VECTOR((tokens, block), jnp.float32),
            DMA((rest // step,)),
        ],
        grant=24 << 20,
    )
    chunk = shaped((vocab_count, half_tokens, block), jnp.bfloat16)
    gain = norm_gain.astype(jnp.float32).reshape(vocab_count, block)
    arrived, gain = fence((partner(given), gain))
    stream = call(
        stream_kernel,
        chunk,
        (kept, arrived),
        [NEAR] * 2,
        [VECTOR(chunk.shape[1:], chunk.dtype), DMA((vocab_count,))],
        SMALL,
        FREE,
    )
    stream, head_rows = fence((stream, head_weight.T))
    early_sizes = (half_width // 2, half_width // 4)
    early = fetched(head_rows, early_sizes)
    stream = lax.all_to_all(stream, "vocab", 0, 0, tiled=True)
    stream, *early = fence((stream, *early))
    part = shaped((half_tokens, half_width), jnp.bfloat16)
    own, other = call(norm_kernel, (part, part), (stream, gain), [NEAR] * 2)
    rest = half_width - sum(early_sizes)
    mine = call(
        head_kernel,
        shaped((tokens, columns_here + 1), jnp.float32),
        (own, partner(other), targets, *early, head_rows),
        [NEAR] * 5 + [FAR],
        [
            VECTOR((columns_here, rest), jnp.bfloat16),
            VECTOR((tokens, half_width), jnp.bfloat16),
            DMA((rest // block_of(rest, 512),)),
        ],
        grant=12 << 20,
    )
    row = shaped((vocab_count, 1, 3 * tokens), jnp.float32)
    stats = call(stats_kernel, row, (mine, partner(mine)), [NEAR] * 2)
    model_count = lax.axis_size("mp")
    mixed = [
        [peer * model_count + (peer + core) % model_count for peer in range(vocab_count)]
        for core in range(model_count)
    ]
    stats, is_low = fence((stats, lax.axis_index("mp") == 0))
    stats = fence(
        lax.all_to_all(stats, ("vocab", "mp"), 0, 0, tiled=True, axis_index_groups=mixed)
    )
    tops, totals, chosen = jnp.split(stats[:, 0], 3, axis=1)
    top = jnp.max(tops, axis=0)
    total = jnp.sum(totals * jnp.exp(tops - top[None]), axis=0)
    chosen = jnp.sum(chosen, axis=0)
    low, high = (
        tuple(one[side] for one in (top, total, chosen))
        for side in (slice(None, half_tokens), slice(half_tokens, None))
    )
    top, total, chosen = (jnp.where(is_low, here, there) for here, there in zip(low, high))
    return chosen - top - jnp.log(total)


def solution(mesh):
    return jax.shard_map(
        body,
        mesh=mesh,
        in_specs=(
            P(("groups", "vocab"), "mp"),
            P(("groups", "vocab"), "mp"),
            P("vocab", "mp"),
            P(("groups", "vocab", "mp"), None),
            P(),
            P("mp", "vocab"),
            P(("groups", "mp")),
        ),
        out_specs=P(("groups", "mp")),
        check_vma=False,
    )
```

```python
import jax
import jax.numpy as jnp
from jax import lax
from jax.experimental import pallas as pl
from jax.experimental.pallas import tpu as pltpu
from jax.sharding import PartitionSpec as P

EPSILON = 1e-05
ROWS_BY_ROWS = (((1,), (1,)), ((), ()))
SMALL = 2 << 20
HEAD_PARTS = 2
fence = lax.optimization_barrier
NEAR = pl.BlockSpec(memory_space=pltpu.VMEM)
FAR = pl.BlockSpec(memory_space=pltpu.HBM)
VECTOR = pltpu.VMEM
DMA = pltpu.SemaphoreType.DMA


def partner(value):
    return lax.ppermute(value, "mp", [(0, 1), (1, 0)])


def swapped(value):
    return fence(lax.all_to_all(fence(value), "vocab", 0, 0, tiled=True))


def call(kernel, out_shape, operands, places, scratch=(), grant=SMALL):
    operands = tuple(
        pltpu.with_memory_space_constraint(one, pltpu.HBM) if place is FAR else one
        for one, place in zip(operands, places)
    )
    return pl.pallas_call(
        kernel,
        out_shape=out_shape,
        in_specs=places,
        out_specs=jax.tree.map(lambda _: NEAR, out_shape),
        scratch_shapes=list(scratch),
        compiler_params=pltpu.CompilerParams(vmem_limit_bytes=grant),
    )(*operands)


def block_of(length, most):
    return max(size for size in range(1, most + 1) if length % size == 0)


def gated_kernel(gate_hbm, up_hbm, residual_hbm, out_ref, gate_ref, up_ref, residual_ref, done):
    loads = (
        pltpu.make_async_copy(gate_hbm, gate_ref, done.at[0]),
        pltpu.make_async_copy(up_hbm, up_ref, done.at[1]),
        pltpu.make_async_copy(residual_hbm, residual_ref, done.at[2]),
    )
    for load in loads:
        load.start()
    for load in loads:
        load.wait()
    count, rows, width = out_ref.shape
    units = gate_ref.shape[1]
    extra = width - units
    gate = gate_ref[...].astype(jnp.float32)
    up = up_ref[...].astype(jnp.float32)
    gated = (gate / (1.0 + jnp.exp(-gate)) * up).astype(jnp.bfloat16)
    for peer in range(count):
        out_ref[peer, :, :units] = gated
        for row in range(rows):
            first = (peer * rows + row) * extra
            out_ref[peer, row : row + 1, units:] = residual_ref[:, first : first + extra]


def weight_loads(weight_hbm, weight_ref, done):
    depth = weight_ref.shape[1] // done.shape[0]
    loads = []
    for part in range(done.shape[0]):
        here = (slice(None), pl.ds(part * depth, depth))
        loads.append(
            pltpu.make_async_copy(weight_hbm.at[here], weight_ref.at[here], done.at[part])
        )
        loads[-1].start()
    return loads


def product(terms, left_ref, weight_ref, loads):
    depth = weight_ref.shape[1] // len(loads)
    for part, load in enumerate(loads):
        load.wait()
        here = slice(part * depth, (part + 1) * depth)
        terms += lax.dot_general(
            left_ref[:, here],
            weight_ref[:, here],
            ROWS_BY_ROWS,
            preferred_element_type=jnp.float32,
        )
    return terms


def down_kernel(chunks_ref, weight_hbm, kept_ref, given_ref, weight_ref, units_ref, own_ref, done):
    loads = weight_loads(weight_hbm, weight_ref, done)
    units = weight_hbm.shape[1]
    count, rows, width = chunks_ref.shape
    half, block = kept_ref.shape
    index = lax.axis_index("mp")
    token = lax.broadcasted_iota(jnp.int32, (rows, block), 0)
    for peer in range(count):
        units_ref[peer * rows : (peer + 1) * rows, :] = chunks_ref[peer, :, :units]
        pieces = [chunks_ref[peer, row : row + 1, units:].astype(jnp.float32) for row in range(rows)]
        residual = jnp.broadcast_to(jnp.concatenate(pieces, axis=1), (rows, block))
        own_ref[peer * rows : (peer + 1) * rows, :] = jnp.where(token == index, residual, 0.0)
    terms = product(own_ref[...], units_ref, weight_ref, loads)
    low, high = terms[:half], terms[half:]
    kept_ref[...] = jnp.where(index == 0, low, high)
    given_ref[...] = jnp.where(index == 0, high, low)


def stream_kernel(kept_ref, arrived_ref, out_ref):
    stream = (kept_ref[...] + arrived_ref[...]).astype(jnp.bfloat16)
    for peer in range(out_ref.shape[0]):
        out_ref[peer] = stream


def norm_kernel(stream_ref, gain_ref, own_ref, other_ref):
    count, tokens, block = stream_ref.shape
    half = count // 2
    squares = jnp.zeros((tokens, block), jnp.float32)
    for part in range(count):
        values = stream_ref[part].astype(jnp.float32)
        squares += values * values
    mean_square = jnp.sum(squares, axis=1, keepdims=True) / (count * block)
    scale = lax.rsqrt(mean_square + EPSILON)
    index = lax.axis_index("mp")
    for out_ref, side in ((own_ref, 1 - index), (other_ref, index)):
        for part in range(half):
            at = side * half + part
            gain = gain_ref[pl.ds(at, 1), :]
            values = stream_ref[at].astype(jnp.float32) * scale * gain
            out_ref[:, part * block : (part + 1) * block] = values.astype(jnp.bfloat16)


def column_of(row_ref):
    size = row_ref.shape[0]
    square = (size, size)
    diagonal = lax.broadcasted_iota(jnp.int32, square, 0) == lax.broadcasted_iota(
        jnp.int32, square, 1
    )
    spread = jnp.broadcast_to(row_ref[...].reshape(1, size), square).astype(jnp.float32)
    return jnp.sum(jnp.where(diagonal, spread, 0.0), axis=1, keepdims=True)


def head_kernel(own_ref, other_ref, targets_ref, weight_ref, out_ref, halves_ref):
    tokens = own_ref.shape[0]
    columns, width = weight_ref.shape
    halves_ref[...] = jnp.concatenate([own_ref[...], other_ref[...]], axis=0)
    out_ref[:tokens, columns:] = column_of(targets_ref)
    out_ref[tokens:, columns:] = jnp.zeros((tokens, 1), jnp.float32)
    terms = jnp.zeros((2 * tokens, columns), jnp.float32)
    depth = width // HEAD_PARTS
    for part in range(HEAD_PARTS):
        here = slice(part * depth, (part + 1) * depth)
        terms += lax.dot_general(
            halves_ref[:, here],
            weight_ref[:, here],
            ROWS_BY_ROWS,
            preferred_element_type=jnp.float32,
        )
    out_ref[:, :columns] = terms


def stats_kernel(mine_ref, arrived_ref, out_ref):
    half = mine_ref.shape[0] // 2
    columns = mine_ref.shape[1] - 1
    own = mine_ref[:half, :] + arrived_ref[half:, :]
    other = mine_ref[half:, :] + arrived_ref[:half, :]
    is_low = lax.axis_index("mp") == 0
    both = jnp.concatenate(
        [jnp.where(is_low, own, other), jnp.where(is_low, other, own)], axis=0
    )
    logits, wanted = both[:, :columns], both[:, columns:].astype(jnp.int32)
    tokens = 2 * half
    wanted -= lax.axis_index("vocab") * columns
    here = lax.broadcasted_iota(jnp.int32, logits.shape, 1) == wanted
    chosen = jnp.sum(jnp.where(here, logits, 0.0), axis=1, keepdims=True)
    top = jnp.max(logits, axis=1, keepdims=True)
    total = jnp.sum(jnp.exp(logits - top), axis=1, keepdims=True)
    lane = lax.broadcasted_iota(jnp.int32, (tokens, 3 * tokens), 1)
    token = lax.broadcasted_iota(jnp.int32, (tokens, 3 * tokens), 0)
    row = jnp.zeros((tokens, 3 * tokens), jnp.float32)
    for place, value in enumerate((top, total, chosen)):
        row = jnp.where(lane == token + place * tokens, value, row)
    row = jnp.sum(row, axis=0, keepdims=True)
    for peer in range(out_ref.shape[0]):
        out_ref[peer] = row


def body(gate_pre, up_pre, down_weight, residual, norm_gain, head_weight, targets):
    vocab_count = lax.axis_size("vocab")
    rows, half_units = gate_pre.shape
    block = down_weight.shape[0]
    tokens = rows * vocab_count
    half_tokens = targets.shape[0]
    half_width, columns_here = head_weight.shape
    shaped = jax.ShapeDtypeStruct
    step = block_of(half_units, 512)
    extra = residual.shape[0] * block // rows
    chunk = shaped((vocab_count, rows, half_units + extra), jnp.bfloat16)
    operands = (gate_pre, up_pre, residual)
    places = [VECTOR(one.shape, one.dtype) for one in operands]
    chunks = swapped(call(gated_kernel, chunk, operands, [FAR] * 3, places + [DMA((3,))]))
    part = shaped((half_tokens, block), jnp.float32)
    kept, given = call(
        down_kernel,
        (part, part),
        (chunks, down_weight),
        [NEAR, FAR],
        [
            VECTOR(down_weight.shape, jnp.bfloat16),
            VECTOR((tokens, half_units), jnp.bfloat16),
            VECTOR((tokens, block), jnp.float32),
            DMA((half_units // step,)),
        ],
        grant=24 << 20,
    )
    chunk = shaped((vocab_count, half_tokens, block), jnp.bfloat16)
    gain = norm_gain.astype(jnp.float32).reshape(vocab_count, block)
    arrived, gain, head_rows = fence((partner(given), gain, head_weight.T))
    head_rows = partner(head_rows)
    stream = swapped(call(stream_kernel, chunk, (kept, arrived), [NEAR] * 2))
    stream, head_rows = fence((stream, head_rows))
    part = shaped((half_tokens, half_width), jnp.bfloat16)
    own, other = call(norm_kernel, (part, part), (stream, gain), [NEAR] * 2)
    mine = call(
        head_kernel,
        shaped((tokens, columns_here + 1), jnp.float32),
        (own, partner(other), targets, head_rows),
        [NEAR] * 4,
        [VECTOR((tokens, half_width), jnp.bfloat16)],
        grant=8 << 20,
    )
    row = shaped((vocab_count, 1, 3 * tokens), jnp.float32)
    stats = call(stats_kernel, row, (mine, partner(mine)), [NEAR] * 2)
    model_count = lax.axis_size("mp")
    mixed = [
        [peer * model_count + (peer + core) % model_count for peer in range(vocab_count)]
        for core in range(model_count)
    ]
    stats, is_low = fence((stats, lax.axis_index("mp") == 0))
    stats = fence(
        lax.all_to_all(stats, ("vocab", "mp"), 0, 0, tiled=True, axis_index_groups=mixed)
    )
    tops, totals, chosen = jnp.split(stats[:, 0], 3, axis=1)
    top = jnp.max(tops, axis=0)
    total = jnp.sum(totals * jnp.exp(tops - top[None]), axis=0)
    chosen = jnp.sum(chosen, axis=0)
    low, high = (
        tuple(one[side] for one in (top, total, chosen))
        for side in (slice(None, half_tokens), slice(half_tokens, None))
    )
    top, total, chosen = (jnp.where(is_low, here, there) for here, there in zip(low, high))
    return chosen - top - jnp.log(total)


def solution(mesh):
    return jax.shard_map(
        body,
        mesh=mesh,
        in_specs=(
            P(("groups", "vocab"), "mp"),
            P(("groups", "vocab"), "mp"),
            P("vocab", "mp"),
            P(("groups", "vocab", "mp"), None),
            P(),
            P("mp", "vocab"),
            P(("groups", "mp")),
        ),
        out_specs=P(("groups", "mp")),
        check_vma=False,
    )
```

```python
import jax
import jax.numpy as jnp
from jax import lax
from jax.experimental import pallas as pl
from jax.experimental.pallas import tpu as pltpu
from jax.sharding import PartitionSpec as P

EPSILON = 1e-05
ROWS_BY_ROWS = (((1,), (1,)), ((), ()))
SMALL = 2 << 20
HEAD_PARTS = 2
fence = lax.optimization_barrier
NEAR = pl.BlockSpec(memory_space=pltpu.VMEM)
FAR = pl.BlockSpec(memory_space=pltpu.HBM)
VECTOR = pltpu.VMEM
DMA = pltpu.SemaphoreType.DMA


def partner(value):
    return lax.ppermute(value, "mp", [(0, 1), (1, 0)])


def swapped(value):
    return fence(lax.all_to_all(fence(value), "vocab", 0, 0, tiled=True))


def call(kernel, out_shape, operands, places, scratch=(), grant=SMALL):
    operands = tuple(
        pltpu.with_memory_space_constraint(one, pltpu.HBM) if place is FAR else one
        for one, place in zip(operands, places)
    )
    return pl.pallas_call(
        kernel,
        out_shape=out_shape,
        in_specs=places,
        out_specs=jax.tree.map(lambda _: NEAR, out_shape),
        scratch_shapes=list(scratch),
        compiler_params=pltpu.CompilerParams(vmem_limit_bytes=grant),
    )(*operands)


def block_of(length, most):
    return max(size for size in range(1, most + 1) if length % size == 0)


def gated_kernel(gate_hbm, up_hbm, residual_hbm, out_ref, gate_ref, up_ref, residual_ref, done):
    loads = (
        pltpu.make_async_copy(gate_hbm, gate_ref, done.at[0]),
        pltpu.make_async_copy(up_hbm, up_ref, done.at[1]),
        pltpu.make_async_copy(residual_hbm, residual_ref, done.at[2]),
    )
    for load in loads:
        load.start()
    for load in loads:
        load.wait()
    count, rows, width = out_ref.shape
    units = gate_ref.shape[1]
    extra = width - units
    gate = gate_ref[...].astype(jnp.float32)
    up = up_ref[...].astype(jnp.float32)
    gated = (gate / (1.0 + jnp.exp(-gate)) * up).astype(jnp.bfloat16)
    for peer in range(count):
        out_ref[peer, :, :units] = gated
        for row in range(rows):
            first = (peer * rows + row) * extra
            out_ref[peer, row : row + 1, units:] = residual_ref[:, first : first + extra]


def weight_loads(weight_hbm, weight_ref, done):
    depth = weight_ref.shape[1] // done.shape[0]
    loads = []
    for part in range(done.shape[0]):
        here = (slice(None), pl.ds(part * depth, depth))
        loads.append(
            pltpu.make_async_copy(weight_hbm.at[here], weight_ref.at[here], done.at[part])
        )
        loads[-1].start()
    return loads


def product(terms, left_ref, weight_ref, loads):
    depth = weight_ref.shape[1] // len(loads)
    for part, load in enumerate(loads):
        load.wait()
        here = slice(part * depth, (part + 1) * depth)
        terms += lax.dot_general(
            left_ref[:, here],
            weight_ref[:, here],
            ROWS_BY_ROWS,
            preferred_element_type=jnp.float32,
        )
    return terms


def down_kernel(chunks_ref, weight_hbm, kept_ref, given_ref, weight_ref, units_ref, own_ref, done):
    loads = weight_loads(weight_hbm, weight_ref, done)
    units = weight_hbm.shape[1]
    count, rows, width = chunks_ref.shape
    half, block = kept_ref.shape
    index = lax.axis_index("mp")
    token = lax.broadcasted_iota(jnp.int32, (rows, block), 0)
    for peer in range(count):
        units_ref[peer * rows : (peer + 1) * rows, :] = chunks_ref[peer, :, :units]
        pieces = [chunks_ref[peer, row : row + 1, units:].astype(jnp.float32) for row in range(rows)]
        residual = jnp.broadcast_to(jnp.concatenate(pieces, axis=1), (rows, block))
        own_ref[peer * rows : (peer + 1) * rows, :] = jnp.where(token == index, residual, 0.0)
    terms = product(own_ref[...], units_ref, weight_ref, loads)
    low, high = terms[:half], terms[half:]
    kept_ref[...] = jnp.where(index == 0, low, high)
    given_ref[...] = jnp.where(index == 0, high, low)


def stream_kernel(kept_ref, arrived_ref, out_ref):
    stream = (kept_ref[...] + arrived_ref[...]).astype(jnp.bfloat16)
    for peer in range(out_ref.shape[0]):
        out_ref[peer] = stream


def column_of(row_ref):
    size = row_ref.shape[0]
    square = (size, size)
    diagonal = lax.broadcasted_iota(jnp.int32, square, 0) == lax.broadcasted_iota(
        jnp.int32, square, 1
    )
    spread = jnp.broadcast_to(row_ref[...].reshape(1, size), square).astype(jnp.float32)
    return jnp.sum(jnp.where(diagonal, spread, 0.0), axis=1, keepdims=True)


def score_kernel(
    stream_ref, gain_ref, targets_ref, other_ref, weight_hbm, out_ref, weight_ref, normed_ref, done
):
    loads = weight_loads(weight_hbm, weight_ref, done)
    count, tokens, block = stream_ref.shape
    columns, width = weight_ref.shape
    blocks = width // block
    squares = jnp.zeros((tokens, block), jnp.float32)
    for part in range(count):
        values = stream_ref[part].astype(jnp.float32)
        squares += values * values
    mean_square = jnp.sum(squares, axis=1, keepdims=True) / (count * block)
    scale = lax.rsqrt(mean_square + EPSILON)
    for part in range(count):
        values = stream_ref[part].astype(jnp.float32) * scale * gain_ref[part : part + 1, :]
        first = part % blocks * block
        normed_ref[part // blocks, :, first : first + block] = values.astype(jnp.bfloat16)
    index = lax.axis_index("mp")
    wanted = column_of(targets_ref).astype(jnp.int32) - lax.axis_index("vocab") * columns
    terms = jnp.zeros((tokens, columns), jnp.float32)
    depth = width // HEAD_PARTS
    for part in range(HEAD_PARTS):
        here = slice(part * depth, (part + 1) * depth)
        terms += lax.dot_general(
            normed_ref[1 - index, :, here],
            other_ref[:, here],
            ROWS_BY_ROWS,
            preferred_element_type=jnp.float32,
        )
    logits = product(terms, normed_ref.at[index], weight_ref, loads)
    here = lax.broadcasted_iota(jnp.int32, logits.shape, 1) == wanted
    chosen = jnp.sum(jnp.where(here, logits, 0.0), axis=1, keepdims=True)
    top = jnp.max(logits, axis=1, keepdims=True)
    total = jnp.sum(jnp.exp(logits - top), axis=1, keepdims=True)
    lane = lax.broadcasted_iota(jnp.int32, (tokens, 3 * tokens), 1)
    token = lax.broadcasted_iota(jnp.int32, (tokens, 3 * tokens), 0)
    row = jnp.zeros((tokens, 3 * tokens), jnp.float32)
    for place, value in enumerate((top, total, chosen)):
        row = jnp.where(lane == token + place * tokens, value, row)
    row = jnp.sum(row, axis=0, keepdims=True)
    for peer in range(out_ref.shape[0]):
        out_ref[peer] = row


def body(gate_pre, up_pre, down_weight, residual, norm_gain, head_weight, targets):
    vocab_count = lax.axis_size("vocab")
    rows, half_units = gate_pre.shape
    block = down_weight.shape[0]
    tokens = rows * vocab_count
    half_tokens = targets.shape[0]
    half_width, columns_here = head_weight.shape
    shaped = jax.ShapeDtypeStruct
    step = block_of(half_units, 512)
    extra = residual.shape[0] * block // rows
    chunk = shaped((vocab_count, rows, half_units + extra), jnp.bfloat16)
    operands = (gate_pre, up_pre, residual)
    places = [VECTOR(one.shape, one.dtype) for one in operands]
    chunks = swapped(call(gated_kernel, chunk, operands, [FAR] * 3, places + [DMA((3,))]))
    part = shaped((half_tokens, block), jnp.float32)
    kept, given = call(
        down_kernel,
        (part, part),
        (chunks, down_weight),
        [NEAR, FAR],
        [
            VECTOR(down_weight.shape, jnp.bfloat16),
            VECTOR((tokens, half_units), jnp.bfloat16),
            VECTOR((tokens, block), jnp.float32),
            DMA((half_units // step,)),
        ],
        grant=24 << 20,
    )
    chunk = shaped((vocab_count, half_tokens, block), jnp.bfloat16)
    gain = norm_gain.astype(jnp.float32).reshape(vocab_count, block)
    arrived, gain, head_rows = fence((partner(given), gain, head_weight.T))
    other_rows = partner(head_rows)
    stream = swapped(call(stream_kernel, chunk, (kept, arrived), [NEAR] * 2))
    stream, other_rows = fence((stream, other_rows))
    step = block_of(half_width, 512)
    row = shaped((vocab_count, 1, 3 * half_tokens), jnp.float32)
    stats = call(
        score_kernel,
        row,
        (stream, gain, targets, other_rows, head_rows),
        [NEAR] * 4 + [FAR],
        [
            VECTOR((columns_here, half_width), jnp.bfloat16),
            VECTOR((2, half_tokens, half_width), jnp.bfloat16),
            DMA((half_width // step,)),
        ],
        grant=12 << 20,
    )
    stats = swapped(stats)
    tops, totals, chosen = jnp.split(stats[:, 0], 3, axis=1)
    top = jnp.max(tops, axis=0)
    total = jnp.sum(totals * jnp.exp(tops - top[None]), axis=0)
    return jnp.sum(chosen, axis=0) - top - jnp.log(total)


def solution(mesh):
    return jax.shard_map(
        body,
        mesh=mesh,
        in_specs=(
            P(("groups", "vocab"), "mp"),
            P(("groups", "vocab"), "mp"),
            P("vocab", "mp"),
            P(("groups", "vocab", "mp"), None),
            P(),
            P("mp", "vocab"),
            P(("groups", "mp")),
        ),
        out_specs=P(("groups", "mp")),
        check_vma=False,
    )
```

```python
import jax
import jax.numpy as jnp
from jax import lax
from jax.experimental import pallas as pl
from jax.experimental.pallas import tpu as pltpu
from jax.sharding import PartitionSpec as P

EPSILON = 1e-05
ROWS_BY_ROWS = (((1,), (1,)), ((), ()))
SMALL = 2 << 20
HEAD_PARTS = 2
fence = lax.optimization_barrier
NEAR = pl.BlockSpec(memory_space=pltpu.VMEM)
FAR = pl.BlockSpec(memory_space=pltpu.HBM)
VECTOR = pltpu.VMEM
DMA = pltpu.SemaphoreType.DMA


def mixed_groups():
    count, cores = lax.axis_size("vocab"), lax.axis_size("mp")
    return [[peer * cores + (peer + core) % cores for peer in range(count)] for core in range(cores)]


def group_index():
    return lax.rem(lax.axis_index("mp") + lax.axis_index("vocab"), 2)


def mixed_swap(value):
    return lax.all_to_all(
        value, ("vocab", "mp"), 0, 0, tiled=True, axis_index_groups=mixed_groups()
    )


def partner(value):
    return lax.ppermute(value, "mp", [(0, 1), (1, 0)])


def swapped(value):
    return fence(lax.all_to_all(fence(value), "vocab", 0, 0, tiled=True))


def call(kernel, out_shape, operands, places, scratch=(), grant=SMALL):
    operands = tuple(
        pltpu.with_memory_space_constraint(one, pltpu.HBM) if place is FAR else one
        for one, place in zip(operands, places)
    )
    return pl.pallas_call(
        kernel,
        out_shape=out_shape,
        in_specs=places,
        out_specs=jax.tree.map(lambda _: NEAR, out_shape),
        scratch_shapes=list(scratch),
        compiler_params=pltpu.CompilerParams(vmem_limit_bytes=grant),
    )(*operands)


def block_of(length, most):
    return max(size for size in range(1, most + 1) if length % size == 0)


def gated_kernel(gate_hbm, up_hbm, residual_hbm, out_ref, gate_ref, up_ref, residual_ref, done):
    loads = (
        pltpu.make_async_copy(gate_hbm, gate_ref, done.at[0]),
        pltpu.make_async_copy(up_hbm, up_ref, done.at[1]),
        pltpu.make_async_copy(residual_hbm, residual_ref, done.at[2]),
    )
    for load in loads:
        load.start()
    for load in loads:
        load.wait()
    count, rows, width = out_ref.shape
    units = gate_ref.shape[1]
    extra = width - units
    gate = gate_ref[...].astype(jnp.float32)
    up = up_ref[...].astype(jnp.float32)
    gated = (gate / (1.0 + jnp.exp(-gate)) * up).astype(jnp.bfloat16)
    for peer in range(count):
        out_ref[peer, :, :units] = gated
        for row in range(rows):
            first = (peer * rows + row) * extra
            out_ref[peer, row : row + 1, units:] = residual_ref[:, first : first + extra]


def weight_loads(weight_hbm, weight_ref, done):
    depth = weight_ref.shape[1] // done.shape[0]
    loads = []
    for part in range(done.shape[0]):
        here = (slice(None), pl.ds(part * depth, depth))
        loads.append(
            pltpu.make_async_copy(weight_hbm.at[here], weight_ref.at[here], done.at[part])
        )
        loads[-1].start()
    return loads


def product(terms, left_ref, weight_ref, loads):
    depth = weight_ref.shape[1] // len(loads)
    for part, load in enumerate(loads):
        load.wait()
        here = slice(part * depth, (part + 1) * depth)
        terms += lax.dot_general(
            left_ref[:, here],
            weight_ref[:, here],
            ROWS_BY_ROWS,
            preferred_element_type=jnp.float32,
        )
    return terms


def down_kernel(chunks_ref, weight_hbm, kept_ref, given_ref, weight_ref, units_ref, own_ref, done):
    loads = weight_loads(weight_hbm, weight_ref, done)
    units = weight_hbm.shape[1]
    count, rows, width = chunks_ref.shape
    half, block = kept_ref.shape
    index = lax.axis_index("mp")
    token = lax.broadcasted_iota(jnp.int32, (rows, block), 0)
    for peer in range(count):
        units_ref[peer * rows : (peer + 1) * rows, :] = chunks_ref[peer, :, :units]
        pieces = [chunks_ref[peer, row : row + 1, units:].astype(jnp.float32) for row in range(rows)]
        residual = jnp.broadcast_to(jnp.concatenate(pieces, axis=1), (rows, block))
        own_ref[peer * rows : (peer + 1) * rows, :] = jnp.where(token == index, residual, 0.0)
    terms = product(own_ref[...], units_ref, weight_ref, loads)
    low, high = terms[:half], terms[half:]
    is_low = group_index() == 0
    kept_ref[...] = jnp.where(is_low, low, high)
    given_ref[...] = jnp.where(is_low, high, low)


def stream_kernel(kept_ref, arrived_ref, out_ref):
    stream = (kept_ref[...] + arrived_ref[...]).astype(jnp.bfloat16)
    for peer in range(out_ref.shape[0]):
        out_ref[peer] = stream


def norm_kernel(stream_ref, gain_ref, own_ref, other_ref):
    count, tokens, block = stream_ref.shape
    half = count // 2
    squares = jnp.zeros((tokens, block), jnp.float32)
    for part in range(count):
        values = stream_ref[part].astype(jnp.float32)
        squares += values * values
    mean_square = jnp.sum(squares, axis=1, keepdims=True) / (count * block)
    scale = lax.rsqrt(mean_square + EPSILON)
    index = lax.axis_index("mp")
    for out_ref, side in ((own_ref, 1 - index), (other_ref, index)):
        for part in range(half):
            at = side * half + part
            gain = gain_ref[pl.ds(at, 1), :]
            values = stream_ref[at].astype(jnp.float32) * scale * gain
            out_ref[:, part * block : (part + 1) * block] = values.astype(jnp.bfloat16)


def column_of(row_ref):
    size = row_ref.shape[0]
    square = (size, size)
    diagonal = lax.broadcasted_iota(jnp.int32, square, 0) == lax.broadcasted_iota(
        jnp.int32, square, 1
    )
    spread = jnp.broadcast_to(row_ref[...].reshape(1, size), square).astype(jnp.float32)
    return jnp.sum(jnp.where(diagonal, spread, 0.0), axis=1, keepdims=True)


def head_kernel(own_ref, other_ref, targets_ref, weight_ref, out_ref, halves_ref):
    tokens = own_ref.shape[0]
    columns, width = weight_ref.shape
    halves_ref[...] = jnp.concatenate([own_ref[...], other_ref[...]], axis=0)
    wanted = column_of(targets_ref)
    mine = group_index() == lax.axis_index("mp")
    out_ref[:tokens, columns:] = jnp.where(mine, wanted, 0.0)
    out_ref[tokens:, columns:] = jnp.where(mine, 0.0, wanted)
    terms = jnp.zeros((2 * tokens, columns), jnp.float32)
    depth = width // HEAD_PARTS
    for part in range(HEAD_PARTS):
        here = slice(part * depth, (part + 1) * depth)
        terms += lax.dot_general(
            halves_ref[:, here],
            weight_ref[:, here],
            ROWS_BY_ROWS,
            preferred_element_type=jnp.float32,
        )
    out_ref[:, :columns] = terms


def stats_kernel(mine_ref, arrived_ref, out_ref):
    half = mine_ref.shape[0] // 2
    columns = mine_ref.shape[1] - 1
    own = mine_ref[:half, :] + arrived_ref[half:, :]
    other = mine_ref[half:, :] + arrived_ref[:half, :]
    is_low = group_index() == 0
    both = jnp.concatenate(
        [jnp.where(is_low, own, other), jnp.where(is_low, other, own)], axis=0
    )
    logits, wanted = both[:, :columns], both[:, columns:].astype(jnp.int32)
    tokens = 2 * half
    wanted -= lax.axis_index("vocab") * columns
    here = lax.broadcasted_iota(jnp.int32, logits.shape, 1) == wanted
    chosen = jnp.sum(jnp.where(here, logits, 0.0), axis=1, keepdims=True)
    top = jnp.max(logits, axis=1, keepdims=True)
    total = jnp.sum(jnp.exp(logits - top), axis=1, keepdims=True)
    lane = lax.broadcasted_iota(jnp.int32, (tokens, 3 * tokens), 1)
    token = lax.broadcasted_iota(jnp.int32, (tokens, 3 * tokens), 0)
    row = jnp.zeros((tokens, 3 * tokens), jnp.float32)
    for place, value in enumerate((top, total, chosen)):
        row = jnp.where(lane == token + place * tokens, value, row)
    row = jnp.sum(row, axis=0, keepdims=True)
    for peer in range(out_ref.shape[0]):
        out_ref[peer] = row


def body(gate_pre, up_pre, down_weight, residual, norm_gain, head_weight, targets):
    vocab_count = lax.axis_size("vocab")
    rows, half_units = gate_pre.shape
    block = down_weight.shape[0]
    tokens = rows * vocab_count
    half_tokens = targets.shape[0]
    half_width, columns_here = head_weight.shape
    shaped = jax.ShapeDtypeStruct
    step = block_of(half_units, 512)
    extra = residual.shape[0] * block // rows
    chunk = shaped((vocab_count, rows, half_units + extra), jnp.bfloat16)
    operands = (gate_pre, up_pre, residual)
    places = [VECTOR(one.shape, one.dtype) for one in operands]
    chunks = swapped(call(gated_kernel, chunk, operands, [FAR] * 3, places + [DMA((3,))]))
    part = shaped((half_tokens, block), jnp.float32)
    kept, given = call(
        down_kernel,
        (part, part),
        (chunks, down_weight),
        [NEAR, FAR],
        [
            VECTOR(down_weight.shape, jnp.bfloat16),
            VECTOR((tokens, half_units), jnp.bfloat16),
            VECTOR((tokens, block), jnp.float32),
            DMA((half_units // step,)),
        ],
        grant=24 << 20,
    )
    chunk = shaped((vocab_count, half_tokens, block), jnp.bfloat16)
    gain = norm_gain.astype(jnp.float32).reshape(vocab_count, block)
    arrived, gain, head_rows = fence((partner(given), gain, head_weight.T))
    head_rows = partner(head_rows)
    stream = fence(call(stream_kernel, chunk, (kept, arrived), [NEAR] * 2))
    stream = mixed_swap(stream)
    stream, head_rows = fence((stream, head_rows))
    part = shaped((half_tokens, half_width), jnp.bfloat16)
    own, other = call(norm_kernel, (part, part), (stream, gain), [NEAR] * 2)
    mine = call(
        head_kernel,
        shaped((tokens, columns_here + 1), jnp.float32),
        (own, partner(other), targets, head_rows),
        [NEAR] * 4,
        [VECTOR((tokens, half_width), jnp.bfloat16)],
        grant=8 << 20,
    )
    row = shaped((vocab_count, 1, 3 * tokens), jnp.float32)
    stats = call(stats_kernel, row, (mine, partner(mine)), [NEAR] * 2)
    stats, is_low = fence((stats, lax.axis_index("mp") == 0))
    stats = fence(mixed_swap(stats))
    tops, totals, chosen = jnp.split(stats[:, 0], 3, axis=1)
    top = jnp.max(tops, axis=0)
    total = jnp.sum(totals * jnp.exp(tops - top[None]), axis=0)
    chosen = jnp.sum(chosen, axis=0)
    low, high = (
        tuple(one[side] for one in (top, total, chosen))
        for side in (slice(None, half_tokens), slice(half_tokens, None))
    )
    top, total, chosen = (jnp.where(is_low, here, there) for here, there in zip(low, high))
    return chosen - top - jnp.log(total)


def solution(mesh):
    return jax.shard_map(
        body,
        mesh=mesh,
        in_specs=(
            P(("groups", "vocab"), "mp"),
            P(("groups", "vocab"), "mp"),
            P("vocab", "mp"),
            P(("groups", "vocab", "mp"), None),
            P(),
            P("mp", "vocab"),
            P(("groups", "mp")),
        ),
        out_specs=P(("groups", "mp")),
        check_vma=False,
    )
```

```python
import jax
import jax.numpy as jnp
from jax import lax
from jax.experimental import pallas as pl
from jax.experimental.pallas import tpu as pltpu
from jax.sharding import PartitionSpec as P

EPSILON = 1e-05
ROWS_BY_ROWS = (((1,), (1,)), ((), ()))
SMALL = 2 << 20
HEAD_PARTS = 2
fence = lax.optimization_barrier
NEAR = pl.BlockSpec(memory_space=pltpu.VMEM)
FAR = pl.BlockSpec(memory_space=pltpu.HBM)
VECTOR = pltpu.VMEM
DMA = pltpu.SemaphoreType.DMA


def partner(value):
    return lax.ppermute(value, "mp", [(0, 1), (1, 0)])


def swapped(value):
    return fence(lax.all_to_all(fence(value), "vocab", 0, 0, tiled=True))


def call(kernel, out_shape, operands, places, scratch=(), grant=SMALL):
    operands = tuple(
        pltpu.with_memory_space_constraint(one, pltpu.HBM) if place is FAR else one
        for one, place in zip(operands, places)
    )
    return pl.pallas_call(
        kernel,
        out_shape=out_shape,
        in_specs=places,
        out_specs=jax.tree.map(lambda _: NEAR, out_shape),
        scratch_shapes=list(scratch),
        compiler_params=pltpu.CompilerParams(vmem_limit_bytes=grant),
    )(*operands)


def block_of(length, most):
    return max(size for size in range(1, most + 1) if length % size == 0)


def gated_kernel(
    gate_hbm, up_hbm, residual_hbm, weight_hbm, out_ref, gate_ref, up_ref, residual_ref, done
):
    loads = (
        pltpu.make_async_copy(gate_hbm, gate_ref, done.at[0]),
        pltpu.make_async_copy(up_hbm, up_ref, done.at[1]),
        pltpu.make_async_copy(residual_hbm, residual_ref, done.at[2]),
    )
    for load in loads:
        load.start()
    for load in loads:
        load.wait()
    count, rows, width = out_ref.shape
    units = gate_ref.shape[1]
    extra = width - units
    gate = gate_ref[...].astype(jnp.float32)
    up = up_ref[...].astype(jnp.float32)
    gated = (gate / (1.0 + jnp.exp(-gate)) * up).astype(jnp.bfloat16)
    for peer in range(count):
        out_ref[peer, :, :units] = gated
        for row in range(rows):
            first = (peer * rows + row) * extra
            out_ref[peer, row : row + 1, units:] = residual_ref[:, first : first + extra]


def weight_loads(weight_hbm, weight_ref, done):
    depth = weight_ref.shape[1] // done.shape[0]
    loads = []
    for part in range(done.shape[0]):
        here = (slice(None), pl.ds(part * depth, depth))
        loads.append(
            pltpu.make_async_copy(weight_hbm.at[here], weight_ref.at[here], done.at[part])
        )
        loads[-1].start()
    return loads


def product(terms, left_ref, weight_ref, loads):
    depth = weight_ref.shape[1] // len(loads)
    for part, load in enumerate(loads):
        load.wait()
        here = slice(part * depth, (part + 1) * depth)
        terms += lax.dot_general(
            left_ref[:, here],
            weight_ref[:, here],
            ROWS_BY_ROWS,
            preferred_element_type=jnp.float32,
        )
    return terms


def down_kernel(chunks_ref, weight_ref, kept_ref, given_ref, units_ref, own_ref):
    units = weight_ref.shape[1]
    count, rows, width = chunks_ref.shape
    half, block = kept_ref.shape
    index = lax.axis_index("mp")
    token = lax.broadcasted_iota(jnp.int32, (rows, block), 0)
    for peer in range(count):
        units_ref[peer * rows : (peer + 1) * rows, :] = chunks_ref[peer, :, :units]
        pieces = [chunks_ref[peer, row : row + 1, units:].astype(jnp.float32) for row in range(rows)]
        residual = jnp.broadcast_to(jnp.concatenate(pieces, axis=1), (rows, block))
        own_ref[peer * rows : (peer + 1) * rows, :] = jnp.where(token == index, residual, 0.0)
    terms = own_ref[...]
    depth = block_of(units, 1024)
    for first in range(0, units, depth):
        terms += lax.dot_general(
            units_ref[:, first : first + depth],
            weight_ref[:, first : first + depth],
            ROWS_BY_ROWS,
            preferred_element_type=jnp.float32,
        )
    low, high = terms[:half], terms[half:]
    kept_ref[...] = jnp.where(index == 0, low, high)
    given_ref[...] = jnp.where(index == 0, high, low)


def stream_kernel(kept_ref, arrived_ref, weight_hbm, out_ref):
    stream = (kept_ref[...] + arrived_ref[...]).astype(jnp.bfloat16)
    for peer in range(out_ref.shape[0]):
        out_ref[peer] = stream


def column_of(row_ref):
    size = row_ref.shape[0]
    square = (size, size)
    diagonal = lax.broadcasted_iota(jnp.int32, square, 0) == lax.broadcasted_iota(
        jnp.int32, square, 1
    )
    spread = jnp.broadcast_to(row_ref[...].reshape(1, size), square).astype(jnp.float32)
    return jnp.sum(jnp.where(diagonal, spread, 0.0), axis=1, keepdims=True)


def score_kernel(
    stream_ref, gain_ref, targets_ref, other_ref, weight_ref, out_ref, normed_ref
):
    count, tokens, block = stream_ref.shape
    columns, width = weight_ref.shape
    blocks = width // block
    squares = jnp.zeros((tokens, block), jnp.float32)
    for part in range(count):
        values = stream_ref[part].astype(jnp.float32)
        squares += values * values
    mean_square = jnp.sum(squares, axis=1, keepdims=True) / (count * block)
    scale = lax.rsqrt(mean_square + EPSILON)
    for part in range(count):
        values = stream_ref[part].astype(jnp.float32) * scale * gain_ref[part : part + 1, :]
        first = part % blocks * block
        normed_ref[part // blocks, :, first : first + block] = values.astype(jnp.bfloat16)
    index = lax.axis_index("mp")
    wanted = column_of(targets_ref).astype(jnp.int32) - lax.axis_index("vocab") * columns
    terms = jnp.zeros((tokens, columns), jnp.float32)
    depth = width // HEAD_PARTS
    for part in range(HEAD_PARTS):
        here = slice(part * depth, (part + 1) * depth)
        for side, half_ref in ((index, weight_ref), (1 - index, other_ref)):
            terms += lax.dot_general(
                normed_ref[side, :, here],
                half_ref[:, here],
                ROWS_BY_ROWS,
                preferred_element_type=jnp.float32,
            )
    logits = terms
    here = lax.broadcasted_iota(jnp.int32, logits.shape, 1) == wanted
    chosen = jnp.sum(jnp.where(here, logits, 0.0), axis=1, keepdims=True)
    top = jnp.max(logits, axis=1, keepdims=True)
    total = jnp.sum(jnp.exp(logits - top), axis=1, keepdims=True)
    lane = lax.broadcasted_iota(jnp.int32, (tokens, 3 * tokens), 1)
    token = lax.broadcasted_iota(jnp.int32, (tokens, 3 * tokens), 0)
    row = jnp.zeros((tokens, 3 * tokens), jnp.float32)
    for place, value in enumerate((top, total, chosen)):
        row = jnp.where(lane == token + place * tokens, value, row)
    row = jnp.sum(row, axis=0, keepdims=True)
    for peer in range(out_ref.shape[0]):
        out_ref[peer] = row


def body(gate_pre, up_pre, down_weight, residual, norm_gain, head_weight, targets):
    vocab_count = lax.axis_size("vocab")
    rows, half_units = gate_pre.shape
    block = down_weight.shape[0]
    tokens = rows * vocab_count
    half_tokens = targets.shape[0]
    half_width, columns_here = head_weight.shape
    shaped = jax.ShapeDtypeStruct
    step = block_of(half_units, 512)
    extra = residual.shape[0] * block // rows
    chunk = shaped((vocab_count, rows, half_units + extra), jnp.bfloat16)
    operands = (gate_pre, up_pre, residual)
    places = [VECTOR(one.shape, one.dtype) for one in operands]
    chunks = swapped(
        call(
            gated_kernel,
            chunk,
            operands + (down_weight,),
            [FAR] * 4,
            places + [DMA((3,))],
        )
    )
    part = shaped((half_tokens, block), jnp.float32)
    kept, given = call(
        down_kernel,
        (part, part),
        (chunks, down_weight),
        [NEAR, NEAR],
        [
            VECTOR((tokens, half_units), jnp.bfloat16),
            VECTOR((tokens, block), jnp.float32),
        ],
        grant=8 << 20,
    )
    chunk = shaped((vocab_count, half_tokens, block), jnp.bfloat16)
    gain = norm_gain.astype(jnp.float32).reshape(vocab_count, block)
    arrived, gain, head_rows = fence((partner(given), gain, head_weight.T))
    other_rows = partner(head_rows)
    stream = swapped(call(stream_kernel, chunk, (kept, arrived, head_rows), [NEAR] * 2 + [FAR]))
    stream, other_rows = fence((stream, other_rows))
    row = shaped((vocab_count, 1, 3 * half_tokens), jnp.float32)
    stats = call(
        score_kernel,
        row,
        (stream, gain, targets, other_rows, head_rows),
        [NEAR] * 5,
        [VECTOR((2, half_tokens, half_width), jnp.bfloat16)],
        grant=8 << 20,
    )
    stats = swapped(stats)
    tops, totals, chosen = jnp.split(stats[:, 0], 3, axis=1)
    top = jnp.max(tops, axis=0)
    total = jnp.sum(totals * jnp.exp(tops - top[None]), axis=0)
    return jnp.sum(chosen, axis=0) - top - jnp.log(total)


def solution(mesh):
    return jax.shard_map(
        body,
        mesh=mesh,
        in_specs=(
            P(("groups", "vocab"), "mp"),
            P(("groups", "vocab"), "mp"),
            P("vocab", "mp"),
            P(("groups", "vocab", "mp"), None),
            P(),
            P("mp", "vocab"),
            P(("groups", "mp")),
        ),
        out_specs=P(("groups", "mp")),
        check_vma=False,
    )
```

```python
import jax
import jax.numpy as jnp
from jax import lax
from jax.experimental import pallas as pl
from jax.experimental.pallas import tpu as pltpu
from jax.sharding import PartitionSpec as P

EPSILON = 1e-05
ROWS_BY_ROWS = (((1,), (1,)), ((), ()))
SMALL = 2 << 20
HEAD_PARTS = 2
fence = lax.optimization_barrier
NEAR = pl.BlockSpec(memory_space=pltpu.VMEM)
FAR = pl.BlockSpec(memory_space=pltpu.HBM)
VECTOR = pltpu.VMEM
DMA = pltpu.SemaphoreType.DMA


def partner(value):
    return lax.ppermute(value, "mp", [(0, 1), (1, 0)])


def swapped(value):
    return fence(lax.all_to_all(fence(value), "vocab", 0, 0, tiled=True))


def call(kernel, out_shape, operands, places, scratch=(), grant=SMALL):
    operands = tuple(
        pltpu.with_memory_space_constraint(one, pltpu.HBM) if place is FAR else one
        for one, place in zip(operands, places)
    )
    return pl.pallas_call(
        kernel,
        out_shape=out_shape,
        in_specs=places,
        out_specs=jax.tree.map(lambda _: NEAR, out_shape),
        scratch_shapes=list(scratch),
        compiler_params=pltpu.CompilerParams(vmem_limit_bytes=grant),
    )(*operands)


def block_of(length, most):
    return max(size for size in range(1, most + 1) if length % size == 0)


def gated_kernel(
    gate_hbm, up_hbm, residual_hbm, weight_hbm, out_ref, gate_ref, up_ref, residual_ref, done
):
    loads = (
        pltpu.make_async_copy(gate_hbm, gate_ref, done.at[0]),
        pltpu.make_async_copy(up_hbm, up_ref, done.at[1]),
        pltpu.make_async_copy(residual_hbm, residual_ref, done.at[2]),
    )
    for load in loads:
        load.start()
    for load in loads:
        load.wait()
    count, rows, width = out_ref.shape
    units = gate_ref.shape[1]
    extra = width - units
    gate = gate_ref[...].astype(jnp.float32)
    up = up_ref[...].astype(jnp.float32)
    gated = (gate / (1.0 + jnp.exp(-gate)) * up).astype(jnp.bfloat16)
    for peer in range(count):
        out_ref[peer, :, :units] = gated
        for row in range(rows):
            first = (peer * rows + row) * extra
            out_ref[peer, row : row + 1, units:] = residual_ref[:, first : first + extra]


def weight_loads(weight_hbm, weight_ref, done):
    depth = weight_ref.shape[1] // done.shape[0]
    loads = []
    for part in range(done.shape[0]):
        here = (slice(None), pl.ds(part * depth, depth))
        loads.append(
            pltpu.make_async_copy(weight_hbm.at[here], weight_ref.at[here], done.at[part])
        )
        loads[-1].start()
    return loads


def product(terms, left_ref, weight_ref, loads):
    depth = weight_ref.shape[1] // len(loads)
    for part, load in enumerate(loads):
        load.wait()
        here = slice(part * depth, (part + 1) * depth)
        terms += lax.dot_general(
            left_ref[:, here],
            weight_ref[:, here],
            ROWS_BY_ROWS,
            preferred_element_type=jnp.float32,
        )
    return terms


def down_kernel(chunks_ref, weight_ref, kept_ref, given_ref, units_ref, own_ref):
    units = weight_ref.shape[1]
    count, rows, width = chunks_ref.shape
    half, block = kept_ref.shape
    index = lax.axis_index("mp")
    terms = jnp.zeros((count * rows, block), jnp.float32)
    depth = block_of(units, 1024)
    for first in range(0, units, depth):
        here = slice(first, first + depth)
        for peer in range(count):
            units_ref[peer * rows : (peer + 1) * rows, here] = chunks_ref[peer, :, here]
        terms += lax.dot_general(
            units_ref[:, here],
            weight_ref[:, here],
            ROWS_BY_ROWS,
            preferred_element_type=jnp.float32,
        )
    token = lax.broadcasted_iota(jnp.int32, (rows, block), 0)
    for peer in range(count):
        pieces = [chunks_ref[peer, row : row + 1, units:].astype(jnp.float32) for row in range(rows)]
        residual = jnp.broadcast_to(jnp.concatenate(pieces, axis=1), (rows, block))
        own_ref[peer * rows : (peer + 1) * rows, :] = jnp.where(token == index, residual, 0.0)
    terms += own_ref[...]
    low, high = terms[:half], terms[half:]
    kept_ref[...] = jnp.where(index == 0, low, high)
    given_ref[...] = jnp.where(index == 0, high, low)


def stream_kernel(kept_ref, arrived_ref, weight_hbm, out_ref):
    stream = (kept_ref[...] + arrived_ref[...]).astype(jnp.bfloat16)
    for peer in range(out_ref.shape[0]):
        out_ref[peer] = stream


def column_of(row_ref):
    size = row_ref.shape[0]
    square = (size, size)
    diagonal = lax.broadcasted_iota(jnp.int32, square, 0) == lax.broadcasted_iota(
        jnp.int32, square, 1
    )
    spread = jnp.broadcast_to(row_ref[...].reshape(1, size), square).astype(jnp.float32)
    return jnp.sum(jnp.where(diagonal, spread, 0.0), axis=1, keepdims=True)


def score_kernel(
    stream_ref, gain_ref, targets_ref, other_ref, weight_ref, out_ref, normed_ref
):
    count, tokens, block = stream_ref.shape
    columns, width = weight_ref.shape
    blocks = width // block
    squares = jnp.zeros((tokens, block), jnp.float32)
    for part in range(count):
        values = stream_ref[part].astype(jnp.float32)
        squares += values * values
    mean_square = jnp.sum(squares, axis=1, keepdims=True) / (count * block)
    scale = lax.rsqrt(mean_square + EPSILON)
    for part in range(count):
        values = stream_ref[part].astype(jnp.float32) * scale * gain_ref[part : part + 1, :]
        first = part % blocks * block
        normed_ref[part // blocks, :, first : first + block] = values.astype(jnp.bfloat16)
    index = lax.axis_index("mp")
    wanted = column_of(targets_ref).astype(jnp.int32) - lax.axis_index("vocab") * columns
    terms = jnp.zeros((tokens, columns), jnp.float32)
    depth = width // HEAD_PARTS
    for part in range(HEAD_PARTS):
        here = slice(part * depth, (part + 1) * depth)
        for side, half_ref in ((index, weight_ref), (1 - index, other_ref)):
            terms += lax.dot_general(
                normed_ref[side, :, here],
                half_ref[:, here],
                ROWS_BY_ROWS,
                preferred_element_type=jnp.float32,
            )
    logits = terms
    here = lax.broadcasted_iota(jnp.int32, logits.shape, 1) == wanted
    chosen = jnp.sum(jnp.where(here, logits, 0.0), axis=1, keepdims=True)
    top = jnp.max(logits, axis=1, keepdims=True)
    total = jnp.sum(jnp.exp(logits - top), axis=1, keepdims=True)
    lane = lax.broadcasted_iota(jnp.int32, (tokens, 3 * tokens), 1)
    token = lax.broadcasted_iota(jnp.int32, (tokens, 3 * tokens), 0)
    row = jnp.zeros((tokens, 3 * tokens), jnp.float32)
    for place, value in enumerate((top, total, chosen)):
        row = jnp.where(lane == token + place * tokens, value, row)
    row = jnp.sum(row, axis=0, keepdims=True)
    for peer in range(out_ref.shape[0]):
        out_ref[peer] = row


def body(gate_pre, up_pre, down_weight, residual, norm_gain, head_weight, targets):
    vocab_count = lax.axis_size("vocab")
    rows, half_units = gate_pre.shape
    block = down_weight.shape[0]
    tokens = rows * vocab_count
    half_tokens = targets.shape[0]
    half_width, columns_here = head_weight.shape
    shaped = jax.ShapeDtypeStruct
    step = block_of(half_units, 512)
    extra = residual.shape[0] * block // rows
    chunk = shaped((vocab_count, rows, half_units + extra), jnp.bfloat16)
    operands = (gate_pre, up_pre, residual)
    places = [VECTOR(one.shape, one.dtype) for one in operands]
    chunks = swapped(
        call(
            gated_kernel,
            chunk,
            operands + (down_weight,),
            [FAR] * 4,
            places + [DMA((3,))],
        )
    )
    part = shaped((half_tokens, block), jnp.float32)
    kept, given = call(
        down_kernel,
        (part, part),
        (chunks, down_weight),
        [NEAR, NEAR],
        [
            VECTOR((tokens, half_units), jnp.bfloat16),
            VECTOR((tokens, block), jnp.float32),
        ],
        grant=8 << 20,
    )
    chunk = shaped((vocab_count, half_tokens, block), jnp.bfloat16)
    gain = norm_gain.astype(jnp.float32).reshape(vocab_count, block)
    arrived, gain, head_rows = fence((partner(given), gain, head_weight.T))
    other_rows = partner(head_rows)
    stream = swapped(call(stream_kernel, chunk, (kept, arrived, head_rows), [NEAR] * 2 + [FAR]))
    stream, other_rows = fence((stream, other_rows))
    row = shaped((vocab_count, 1, 3 * half_tokens), jnp.float32)
    stats = call(
        score_kernel,
        row,
        (stream, gain, targets, other_rows, head_rows),
        [NEAR] * 5,
        [VECTOR((2, half_tokens, half_width), jnp.bfloat16)],
        grant=8 << 20,
    )
    stats = swapped(stats)
    tops, totals, chosen = jnp.split(stats[:, 0], 3, axis=1)
    top = jnp.max(tops, axis=0)
    total = jnp.sum(totals * jnp.exp(tops - top[None]), axis=0)
    return jnp.sum(chosen, axis=0) - top - jnp.log(total)


def solution(mesh):
    return jax.shard_map(
        body,
        mesh=mesh,
        in_specs=(
            P(("groups", "vocab"), "mp"),
            P(("groups", "vocab"), "mp"),
            P("vocab", "mp"),
            P(("groups", "vocab", "mp"), None),
            P(),
            P("mp", "vocab"),
            P(("groups", "mp")),
        ),
        out_specs=P(("groups", "mp")),
        check_vma=False,
    )
```

```python
import jax
import jax.numpy as jnp
from jax import lax
from jax.experimental import pallas as pl
from jax.experimental.pallas import tpu as pltpu
from jax.sharding import PartitionSpec as P

EPSILON = 1e-05
ROWS_BY_ROWS = (((1,), (1,)), ((), ()))
SMALL = 2 << 20
HEAD_PARTS = 4
fence = lax.optimization_barrier
NEAR = pl.BlockSpec(memory_space=pltpu.VMEM)
FAR = pl.BlockSpec(memory_space=pltpu.HBM)
VECTOR = pltpu.VMEM
DMA = pltpu.SemaphoreType.DMA


def partner(value):
    return lax.ppermute(value, "mp", [(0, 1), (1, 0)])


def swapped(value):
    return fence(lax.all_to_all(fence(value), "vocab", 0, 0, tiled=True))


def call(kernel, out_shape, operands, places, scratch=(), grant=SMALL):
    operands = tuple(
        pltpu.with_memory_space_constraint(one, pltpu.HBM) if place is FAR else one
        for one, place in zip(operands, places)
    )
    return pl.pallas_call(
        kernel,
        out_shape=out_shape,
        in_specs=places,
        out_specs=jax.tree.map(lambda _: NEAR, out_shape),
        scratch_shapes=list(scratch),
        compiler_params=pltpu.CompilerParams(vmem_limit_bytes=grant),
    )(*operands)


def block_of(length, most):
    return max(size for size in range(1, most + 1) if length % size == 0)


def gated_kernel(
    gate_hbm, up_hbm, residual_hbm, weight_hbm, out_ref, gate_ref, up_ref, residual_ref, done
):
    loads = (
        pltpu.make_async_copy(gate_hbm, gate_ref, done.at[0]),
        pltpu.make_async_copy(up_hbm, up_ref, done.at[1]),
        pltpu.make_async_copy(residual_hbm, residual_ref, done.at[2]),
    )
    for load in loads:
        load.start()
    for load in loads:
        load.wait()
    count, rows, width = out_ref.shape
    units = gate_ref.shape[1]
    extra = width - units
    gate = gate_ref[...].astype(jnp.float32)
    up = up_ref[...].astype(jnp.float32)
    gated = (gate / (1.0 + jnp.exp(-gate)) * up).astype(jnp.bfloat16)
    for peer in range(count):
        out_ref[peer, :, :units] = gated
        for row in range(rows):
            first = (peer * rows + row) * extra
            out_ref[peer, row : row + 1, units:] = residual_ref[:, first : first + extra]


def weight_loads(weight_hbm, weight_ref, done):
    depth = weight_ref.shape[1] // done.shape[0]
    loads = []
    for part in range(done.shape[0]):
        here = (slice(None), pl.ds(part * depth, depth))
        loads.append(
            pltpu.make_async_copy(weight_hbm.at[here], weight_ref.at[here], done.at[part])
        )
        loads[-1].start()
    return loads


def product(terms, left_ref, weight_ref, loads):
    depth = weight_ref.shape[1] // len(loads)
    for part, load in enumerate(loads):
        load.wait()
        here = slice(part * depth, (part + 1) * depth)
        terms += lax.dot_general(
            left_ref[:, here],
            weight_ref[:, here],
            ROWS_BY_ROWS,
            preferred_element_type=jnp.float32,
        )
    return terms


def down_kernel(chunks_ref, weight_ref, kept_ref, given_ref, units_ref, own_ref):
    units = weight_ref.shape[1]
    count, rows, width = chunks_ref.shape
    half, block = kept_ref.shape
    index = lax.axis_index("mp")
    token = lax.broadcasted_iota(jnp.int32, (rows, block), 0)
    for peer in range(count):
        units_ref[peer * rows : (peer + 1) * rows, :] = chunks_ref[peer, :, :units]
        pieces = [chunks_ref[peer, row : row + 1, units:].astype(jnp.float32) for row in range(rows)]
        residual = jnp.broadcast_to(jnp.concatenate(pieces, axis=1), (rows, block))
        own_ref[peer * rows : (peer + 1) * rows, :] = jnp.where(token == index, residual, 0.0)
    terms = own_ref[...]
    depth = block_of(units, 1792)
    for first in range(0, units, depth):
        terms += lax.dot_general(
            units_ref[:, first : first + depth],
            weight_ref[:, first : first + depth],
            ROWS_BY_ROWS,
            preferred_element_type=jnp.float32,
        )
    low, high = terms[:half], terms[half:]
    kept_ref[...] = jnp.where(index == 0, low, high)
    given_ref[...] = jnp.where(index == 0, high, low)


def stream_kernel(kept_ref, arrived_ref, weight_hbm, out_ref):
    stream = (kept_ref[...] + arrived_ref[...]).astype(jnp.bfloat16)
    for peer in range(out_ref.shape[0]):
        out_ref[peer] = stream


def column_of(row_ref):
    size = row_ref.shape[0]
    square = (size, size)
    diagonal = lax.broadcasted_iota(jnp.int32, square, 0) == lax.broadcasted_iota(
        jnp.int32, square, 1
    )
    spread = jnp.broadcast_to(row_ref[...].reshape(1, size), square).astype(jnp.float32)
    return jnp.sum(jnp.where(diagonal, spread, 0.0), axis=1, keepdims=True)


def score_kernel(
    stream_ref, gain_ref, targets_ref, other_ref, weight_ref, out_ref, normed_ref
):
    count, tokens, block = stream_ref.shape
    columns, width = weight_ref.shape
    blocks = width // block
    squares = jnp.zeros((tokens, block), jnp.float32)
    for part in range(count):
        values = stream_ref[part].astype(jnp.float32)
        squares += values * values
    mean_square = jnp.sum(squares, axis=1, keepdims=True) / (count * block)
    scale = lax.rsqrt(mean_square + EPSILON)
    for part in range(count):
        values = stream_ref[part].astype(jnp.float32) * scale * gain_ref[part : part + 1, :]
        first = part % blocks * block
        normed_ref[part // blocks, :, first : first + block] = values.astype(jnp.bfloat16)
    index = lax.axis_index("mp")
    wanted = column_of(targets_ref).astype(jnp.int32) - lax.axis_index("vocab") * columns
    terms = jnp.zeros((tokens, columns), jnp.float32)
    depth = width // HEAD_PARTS
    for part in range(HEAD_PARTS):
        here = slice(part * depth, (part + 1) * depth)
        for side, half_ref in ((index, weight_ref), (1 - index, other_ref)):
            terms += lax.dot_general(
                normed_ref[side, :, here],
                half_ref[:, here],
                ROWS_BY_ROWS,
                preferred_element_type=jnp.float32,
            )
    logits = terms
    here = lax.broadcasted_iota(jnp.int32, logits.shape, 1) == wanted
    chosen = jnp.sum(jnp.where(here, logits, 0.0), axis=1, keepdims=True)
    top = jnp.max(logits, axis=1, keepdims=True)
    total = jnp.sum(jnp.exp(logits - top), axis=1, keepdims=True)
    lane = lax.broadcasted_iota(jnp.int32, (tokens, 3 * tokens), 1)
    token = lax.broadcasted_iota(jnp.int32, (tokens, 3 * tokens), 0)
    row = jnp.zeros((tokens, 3 * tokens), jnp.float32)
    for place, value in enumerate((top, total, chosen)):
        row = jnp.where(lane == token + place * tokens, value, row)
    row = jnp.sum(row, axis=0, keepdims=True)
    for peer in range(out_ref.shape[0]):
        out_ref[peer] = row


def body(gate_pre, up_pre, down_weight, residual, norm_gain, head_weight, targets):
    vocab_count = lax.axis_size("vocab")
    rows, half_units = gate_pre.shape
    block = down_weight.shape[0]
    tokens = rows * vocab_count
    half_tokens = targets.shape[0]
    half_width, columns_here = head_weight.shape
    shaped = jax.ShapeDtypeStruct
    step = block_of(half_units, 512)
    extra = residual.shape[0] * block // rows
    chunk = shaped((vocab_count, rows, half_units + extra), jnp.bfloat16)
    operands = (gate_pre, up_pre, residual)
    places = [VECTOR(one.shape, one.dtype) for one in operands]
    chunks = swapped(
        call(
            gated_kernel,
            chunk,
            operands + (down_weight,),
            [FAR] * 4,
            places + [DMA((3,))],
        )
    )
    part = shaped((half_tokens, block), jnp.float32)
    kept, given = call(
        down_kernel,
        (part, part),
        (chunks, down_weight),
        [NEAR, NEAR],
        [
            VECTOR((tokens, half_units), jnp.bfloat16),
            VECTOR((tokens, block), jnp.float32),
        ],
        grant=8 << 20,
    )
    chunk = shaped((vocab_count, half_tokens, block), jnp.bfloat16)
    gain = norm_gain.astype(jnp.float32).reshape(vocab_count, block)
    arrived, gain, head_rows = fence((partner(given), gain, head_weight.T))
    other_rows = partner(head_rows)
    stream = swapped(call(stream_kernel, chunk, (kept, arrived, head_rows), [NEAR] * 2 + [FAR]))
    stream, other_rows = fence((stream, other_rows))
    row = shaped((vocab_count, 1, 3 * half_tokens), jnp.float32)
    stats = call(
        score_kernel,
        row,
        (stream, gain, targets, other_rows, head_rows),
        [NEAR] * 5,
        [VECTOR((2, half_tokens, half_width), jnp.bfloat16)],
        grant=8 << 20,
    )
    stats = swapped(stats)
    tops, totals, chosen = jnp.split(stats[:, 0], 3, axis=1)
    top = jnp.max(tops, axis=0)
    total = jnp.sum(totals * jnp.exp(tops - top[None]), axis=0)
    return jnp.sum(chosen, axis=0) - top - jnp.log(total)


def solution(mesh):
    return jax.shard_map(
        body,
        mesh=mesh,
        in_specs=(
            P(("groups", "vocab"), "mp"),
            P(("groups", "vocab"), "mp"),
            P("vocab", "mp"),
            P(("groups", "vocab", "mp"), None),
            P(),
            P("mp", "vocab"),
            P(("groups", "mp")),
        ),
        out_specs=P(("groups", "mp")),
        check_vma=False,
    )
```

```python
import jax
import jax.numpy as jnp
from jax import lax
from jax.experimental import pallas as pl
from jax.experimental.pallas import tpu as pltpu
from jax.sharding import PartitionSpec as P

EPSILON = 1e-05
ROWS_BY_ROWS = (((1,), (1,)), ((), ()))
SMALL = 2 << 20
HEAD_PARTS = 2
fence = lax.optimization_barrier
NEAR = pl.BlockSpec(memory_space=pltpu.VMEM)
FAR = pl.BlockSpec(memory_space=pltpu.HBM)
VECTOR = pltpu.VMEM
DMA = pltpu.SemaphoreType.DMA


def partner(value):
    return lax.ppermute(value, "mp", [(0, 1), (1, 0)])


def swapped(value):
    return fence(lax.all_to_all(fence(value), "vocab", 0, 0, tiled=True))


def call(kernel, out_shape, operands, places, scratch=(), grant=SMALL):
    operands = tuple(
        pltpu.with_memory_space_constraint(one, pltpu.HBM) if place is FAR else one
        for one, place in zip(operands, places)
    )
    return pl.pallas_call(
        kernel,
        out_shape=out_shape,
        in_specs=places,
        out_specs=jax.tree.map(lambda _: NEAR, out_shape),
        scratch_shapes=list(scratch),
        compiler_params=pltpu.CompilerParams(vmem_limit_bytes=grant),
    )(*operands)


def block_of(length, most):
    return max(size for size in range(1, most + 1) if length % size == 0)


def gated_kernel(
    gate_hbm, up_hbm, residual_hbm, weight_hbm, out_ref, gate_ref, up_ref, residual_ref, done
):
    loads = (
        pltpu.make_async_copy(gate_hbm, gate_ref, done.at[0]),
        pltpu.make_async_copy(up_hbm, up_ref, done.at[1]),
        pltpu.make_async_copy(residual_hbm, residual_ref, done.at[2]),
    )
    for load in loads:
        load.start()
    for load in loads:
        load.wait()
    count, rows, width = out_ref.shape
    units = gate_ref.shape[1]
    extra = width - units
    gate = gate_ref[...].astype(jnp.float32)
    up = up_ref[...].astype(jnp.float32)
    gated = (gate / (1.0 + jnp.exp(-gate)) * up).astype(jnp.bfloat16)
    for peer in range(count):
        out_ref[peer, :, :units] = gated
        for row in range(rows):
            first = (peer * rows + row) * extra
            out_ref[peer, row : row + 1, units:] = residual_ref[:, first : first + extra]


def weight_loads(weight_hbm, weight_ref, done):
    depth = weight_ref.shape[1] // done.shape[0]
    loads = []
    for part in range(done.shape[0]):
        here = (slice(None), pl.ds(part * depth, depth))
        loads.append(
            pltpu.make_async_copy(weight_hbm.at[here], weight_ref.at[here], done.at[part])
        )
        loads[-1].start()
    return loads


def product(terms, left_ref, weight_ref, loads):
    depth = weight_ref.shape[1] // len(loads)
    for part, load in enumerate(loads):
        load.wait()
        here = slice(part * depth, (part + 1) * depth)
        terms += lax.dot_general(
            left_ref[:, here],
            weight_ref[:, here],
            ROWS_BY_ROWS,
            preferred_element_type=jnp.float32,
        )
    return terms


def down_kernel(chunks_ref, weight_ref, kept_ref, given_ref, units_ref, own_ref):
    units = weight_ref.shape[1]
    count, rows, width = chunks_ref.shape
    half, block = kept_ref.shape
    index = lax.axis_index("mp")
    token = lax.broadcasted_iota(jnp.int32, (rows, block), 0)
    for peer in range(count):
        units_ref[peer * rows : (peer + 1) * rows, :] = chunks_ref[peer, :, :units]
        pieces = [chunks_ref[peer, row : row + 1, units:].astype(jnp.float32) for row in range(rows)]
        residual = jnp.broadcast_to(jnp.concatenate(pieces, axis=1), (rows, block))
        own_ref[peer * rows : (peer + 1) * rows, :] = jnp.where(token == index, residual, 0.0)
    terms = own_ref[...]
    depth = block_of(units, 1024)
    for first in range(0, units, depth):
        terms += lax.dot_general(
            units_ref[:, first : first + depth],
            weight_ref[:, first : first + depth],
            ROWS_BY_ROWS,
            preferred_element_type=jnp.float32,
        )
    low, high = terms[:half], terms[half:]
    kept_ref[...] = jnp.where(index == 0, low, high)
    given_ref[...] = jnp.where(index == 0, high, low)


def stream_kernel(kept_ref, arrived_ref, weight_hbm, out_ref):
    stream = (kept_ref[...] + arrived_ref[...]).astype(jnp.bfloat16)
    for peer in range(out_ref.shape[0]):
        out_ref[peer] = stream


def column_of(row_ref):
    size = row_ref.shape[0]
    square = (size, size)
    diagonal = lax.broadcasted_iota(jnp.int32, square, 0) == lax.broadcasted_iota(
        jnp.int32, square, 1
    )
    spread = jnp.broadcast_to(row_ref[...].reshape(1, size), square).astype(jnp.float32)
    return jnp.sum(jnp.where(diagonal, spread, 0.0), axis=1, keepdims=True)


def score_kernel(
    stream_ref, gain_ref, targets_ref, other_ref, weight_ref, out_ref, normed_ref
):
    count, tokens, block = stream_ref.shape
    columns, width = weight_ref.shape
    blocks = width // block
    squares = jnp.zeros((tokens, block), jnp.float32)
    for part in range(count):
        values = stream_ref[part].astype(jnp.float32)
        squares += values * values
    mean_square = jnp.sum(squares, axis=1, keepdims=True) / (count * block)
    scale = lax.rsqrt(mean_square + EPSILON)
    for part in range(count):
        gain = gain_ref[part * block : (part + 1) * block].astype(jnp.float32).reshape(1, block)
        values = stream_ref[part].astype(jnp.float32) * scale * gain
        first = part % blocks * block
        normed_ref[part // blocks, :, first : first + block] = values.astype(jnp.bfloat16)
    index = lax.axis_index("mp")
    wanted = column_of(targets_ref).astype(jnp.int32) - lax.axis_index("vocab") * columns
    terms = jnp.zeros((tokens, columns), jnp.float32)
    depth = width // HEAD_PARTS
    for part in range(HEAD_PARTS):
        here = slice(part * depth, (part + 1) * depth)
        for side, half_ref in ((index, weight_ref), (1 - index, other_ref)):
            terms += lax.dot_general(
                normed_ref[side, :, here],
                half_ref[:, here],
                ROWS_BY_ROWS,
                preferred_element_type=jnp.float32,
            )
    logits = terms
    here = lax.broadcasted_iota(jnp.int32, logits.shape, 1) == wanted
    chosen = jnp.sum(jnp.where(here, logits, 0.0), axis=1, keepdims=True)
    top = jnp.max(logits, axis=1, keepdims=True)
    total = jnp.sum(jnp.exp(logits - top), axis=1, keepdims=True)
    lane = lax.broadcasted_iota(jnp.int32, (tokens, 3 * tokens), 1)
    token = lax.broadcasted_iota(jnp.int32, (tokens, 3 * tokens), 0)
    row = jnp.zeros((tokens, 3 * tokens), jnp.float32)
    for place, value in enumerate((top, total, chosen)):
        row = jnp.where(lane == token + place * tokens, value, row)
    row = jnp.sum(row, axis=0, keepdims=True)
    for peer in range(out_ref.shape[0]):
        out_ref[peer] = row


def body(gate_pre, up_pre, down_weight, residual, norm_gain, head_weight, targets):
    vocab_count = lax.axis_size("vocab")
    rows, half_units = gate_pre.shape
    block = down_weight.shape[0]
    tokens = rows * vocab_count
    half_tokens = targets.shape[0]
    half_width, columns_here = head_weight.shape
    shaped = jax.ShapeDtypeStruct
    step = block_of(half_units, 512)
    extra = residual.shape[0] * block // rows
    chunk = shaped((vocab_count, rows, half_units + extra), jnp.bfloat16)
    operands = (gate_pre, up_pre, residual)
    places = [VECTOR(one.shape, one.dtype) for one in operands]
    chunks = swapped(
        call(
            gated_kernel,
            chunk,
            operands + (down_weight,),
            [FAR] * 4,
            places + [DMA((3,))],
        )
    )
    chunks, head_rows = fence((chunks, head_weight.T))
    other_rows = partner(head_rows)
    part = shaped((half_tokens, block), jnp.float32)
    kept, given = call(
        down_kernel,
        (part, part),
        (chunks, down_weight),
        [NEAR, NEAR],
        [
            VECTOR((tokens, half_units), jnp.bfloat16),
            VECTOR((tokens, block), jnp.float32),
        ],
        grant=8 << 20,
    )
    chunk = shaped((vocab_count, half_tokens, block), jnp.bfloat16)
    arrived = partner(given)
    stream = swapped(call(stream_kernel, chunk, (kept, arrived, head_rows), [NEAR] * 2 + [FAR]))
    stream, other_rows = fence((stream, other_rows))
    row = shaped((vocab_count, 1, 3 * half_tokens), jnp.float32)
    stats = call(
        score_kernel,
        row,
        (stream, norm_gain, targets, other_rows, head_rows),
        [NEAR] * 5,
        [VECTOR((2, half_tokens, half_width), jnp.bfloat16)],
        grant=8 << 20,
    )
    stats = swapped(stats)
    tops, totals, chosen = jnp.split(stats[:, 0], 3, axis=1)
    top = jnp.max(tops, axis=0)
    total = jnp.sum(totals * jnp.exp(tops - top[None]), axis=0)
    return jnp.sum(chosen, axis=0) - top - jnp.log(total)


def solution(mesh):
    return jax.shard_map(
        body,
        mesh=mesh,
        in_specs=(
            P(("groups", "vocab"), "mp"),
            P(("groups", "vocab"), "mp"),
            P("vocab", "mp"),
            P(("groups", "vocab", "mp"), None),
            P(),
            P("mp", "vocab"),
            P(("groups", "mp")),
        ),
        out_specs=P(("groups", "mp")),
        check_vma=False,
    )
```
